32 devices in a mesh: seq: 8 (over z, x), head: 4 (over y, core).
Axes of the slice: x: 2, y: 2, z: 4, core: 2. Of those that a mesh axis runs over, the one named last changes fastest.
Arguments:
- queries: bfloat16 [3072, 1536], P('seq', 'head'), may hold values from -6 to 6
- key_vectors: bfloat16 [3072, 1536], P('seq', 'head'), may hold values from -6 to 6
- value_vectors: bfloat16 [3072, 1536], P('seq', 'head'), may hold values from -6 to 6
- out_weight: bfloat16 [1536, 5120], P('head'), may hold values from -0.15625 to 0.15625
- d_output: bfloat16 [3072, 5120], P('seq', 'head'), may hold values from -6 to 6
- block_keys: int32 [24, 24], replicated, may hold values from 0 to 23, as said below
- key_count: int32 [24], replicated, may hold values from 12 to 24
- frame_slot: int32 [8], replicated, may hold values from 0 to 7, each once
Outputs:
- layer_out: bfloat16 [3072, 5120], P('seq', 'head')
- d_query: bfloat16 [3072, 1536], P('seq', 'head')
- d_key: bfloat16 [3072, 1536], P('seq', 'head')
- d_value: bfloat16 [3072, 1536], P('seq', 'head')
- d_weight: bfloat16 [1536, 5120], P('head', 'seq')
The draws below stay inside these ranges and needn't reach their ends.
Inputs may be any that keep to these rules, and one draw needn't show every extreme that they name: `block_keys`: row l names distinct logical key blocks for the logical query block l; the first 3 entries are the blocks of the query's own frame, the query block itself first; only the first key_count[l] entries are attended.
All inputs are finite; a program needn't handle non-finite values.
Results may differ from the reference program's by a relative error of at most 0.018.
Values may be sent and summed in bfloat16 or wider, within the bound.
A program may use at most 192 MiB of HBM per device.

```python
import math
import jax
import jax.numpy as jnp
from jax import lax

D = 5120
HD = 128
HEAD_DEV = 3
BLOCK = 128
FRAME_TOK = 384
NKB = 24
T_DEV = 384
FRAMES = 8
TOKENS = 3072
HEADS = 12
N_SEQ = 8
N_HEAD = 4


def drawn_pair(key):
    base_key = jax.random.fold_in(key, 41)
    shape = (TOKENS, HEADS * HD)
    query_draw = jnp.clip(jax.random.normal(jax.random.fold_in(base_key, 1), shape, jnp.float32), -6.0, 6.0)
    key_draw = jnp.clip(jax.random.normal(jax.random.fold_in(base_key, 2), shape, jnp.float32), -6.0, 6.0)
    return (query_draw, key_draw)


def draw_queries(key, part):
    return drawn_pair(key)[0].astype(jnp.bfloat16)


def draw_key_vectors(key, part):
    return drawn_pair(key)[1].astype(jnp.bfloat16)


def radial_lists(key):
    base_key = jax.random.fold_in(key, 23)
    block_count = TOKENS // BLOCK
    per_frame = FRAME_TOK // BLOCK
    block_ids = jnp.arange(block_count, dtype=jnp.int32)
    distance = jnp.abs((block_ids // per_frame)[:, None] - (block_ids // per_frame)[None, :])
    noise = jax.random.randint(jax.random.fold_in(base_key, 1), (block_count, block_count), 0, 4096)
    priority = noise // (1 + distance * distance)
    tiebreak = block_count - 1 - block_ids[None, :]
    ranking = priority * block_count + tiebreak
    ranking = jnp.where(distance == 0, (1 << 22) + tiebreak, ranking)
    ranking = jnp.where(block_ids[:, None] == block_ids[None, :], 1 << 23, ranking)
    ignored, chosen = lax.top_k(ranking, NKB)
    counts = jax.random.randint(jax.random.fold_in(base_key, 2), (block_count,), NKB // 2, NKB + 1)
    fullest = jax.random.randint(jax.random.fold_in(base_key, 3), (), 0, block_count)
    counts = jnp.where(block_ids == fullest, NKB, counts)
    return (chosen.astype(jnp.int32), counts.astype(jnp.int32))


def draw_block_keys(key, part):
    return radial_lists(key)[0]


def draw_key_count(key, part):
    return radial_lists(key)[1]


def strengthened(array, key, source, target, blocks, factor):
    owner, partner = [(jnp.arange(array.shape[position]) // (array.shape[position] // blocks)).reshape([-1 if axis == position else 1 for axis in range(array.ndim)]) for position in (source, target)]
    chosen = jax.random.permutation(key, blocks)[partner]
    strong = (owner == chosen) | (owner == (partner + blocks // 2) % blocks)
    return jnp.where(strong, factor * array, array)


def shard_levels(key, extent, cuts, least, largest):
    level = 1.0
    for dim, parts in cuts:
        heights = jax.random.uniform(jax.random.fold_in(jax.random.fold_in(key, 6), dim), (parts,), jnp.float32, least / len(cuts), largest / len(cuts))
        level = level * jnp.repeat(jnp.exp(heights), extent[dim] // parts).reshape((-1,) + (1,) * (len(extent) - 1 - dim))
    return level


def gaussian(stream_key, extent, scale, limit, pieces=(), kind=jnp.bfloat16):
    level = shard_levels(stream_key, extent, pieces, -0.22, 0.18) if pieces else 1.0
    values = jax.random.normal(stream_key, extent, jnp.float32) * scale * level
    return jnp.minimum(jnp.maximum(values, -limit), limit).astype(kind)


def gaussian_with(rng, shape, scale, most, shards, heavy, kind=jnp.bfloat16):
    values = scale * jax.random.normal(rng, shape, jnp.float32)
    if shards:
        values = values * shard_levels(rng, shape, shards, -0.22, 0.18)
    return jnp.clip(strengthened(values, jax.random.fold_in(rng, 3), *heavy), -most, most).astype(kind)


def setup_inputs(seed: int = 0) -> dict:
    streams_of = jax.random.split(jax.random.key(seed), 9)
    queries = draw_queries(jax.random.fold_in(streams_of[8], 71), 0)
    key_vectors = draw_key_vectors(jax.random.fold_in(streams_of[8], 71), 0)
    value_vectors = gaussian(streams_of[2], (TOKENS, HEADS * HD), 1.0, 6.0, ((0, 8), (1, 4)))
    out_weight = gaussian(streams_of[3], (HEADS * HD, D), (HEADS * HD) ** -0.5, 0.15625, ((0, 4),))
    d_output = gaussian_with(streams_of[4], (TOKENS, D), 1.0, 6.0, ((0, 8), (1, 4)), (0, 1, 8, 2.0))
    block_keys = draw_block_keys(jax.random.fold_in(streams_of[8], 71), 0)
    key_count = draw_key_count(jax.random.fold_in(streams_of[8], 71), 0)
    frame_slot = jax.random.permutation(streams_of[7], FRAMES).astype(jnp.int32)
    return dict(queries=queries, key_vectors=key_vectors, value_vectors=value_vectors, out_weight=out_weight, d_output=d_output, block_keys=block_keys, key_count=key_count, frame_slot=frame_slot)


def rounded(values):
    return lax.optimization_barrier(values.astype(jnp.bfloat16)).astype(jnp.float32)

def storage_lists(block_keys, key_count, frame_slot):
    per_frame = FRAME_TOK // BLOCK
    frames = frame_slot.shape[0]
    block_count = block_keys.shape[0]
    frame_at = jnp.zeros((frames,), jnp.int32).at[frame_slot].set(jnp.arange(frames, dtype=jnp.int32))
    block_ids = jnp.arange(block_count, dtype=jnp.int32)
    logical = frame_at[block_ids // per_frame] * per_frame + block_ids % per_frame
    entries = block_keys[logical]
    counts = key_count[logical]
    stored = frame_slot[entries // per_frame] * per_frame + entries % per_frame
    return (stored.astype(jnp.int32), counts.astype(jnp.int32))

def reference(queries, key_vectors, value_vectors, out_weight, d_output, block_keys, key_count, frame_slot):
    col_count = queries.shape[1]
    head_count = col_count // HD
    block_count = block_keys.shape[0]
    score_scale = 1.0 / math.sqrt(HD)
    stored, counts = storage_lists(block_keys, key_count, frame_slot)
    d_attn = jnp.dot(d_output, out_weight.T, preferred_element_type=jnp.float32).astype(jnp.bfloat16)
    key_blocks = key_vectors.reshape(block_count, BLOCK, head_count, HD)
    value_blocks = value_vectors.reshape(block_count, BLOCK, head_count, HD)
    per_group = T_DEV // BLOCK
    key_span = NKB * BLOCK

    def one_group(carried, inputs):
        key_accum, value_accum = carried
        group_query, group_grad, group_lists, group_counts = inputs
        selected_keys = key_blocks[group_lists].reshape(per_group, key_span, head_count, HD).astype(jnp.float32)
        selected_values = value_blocks[group_lists].reshape(per_group, key_span, head_count, HD).astype(jnp.float32)
        valid_keys = jnp.repeat(jnp.arange(NKB)[None, :] < group_counts[:, None], BLOCK, axis=1)
        query_full = group_query.astype(jnp.float32)
        scores = jnp.einsum('bqhd,bkhd->bhqk', query_full, selected_keys) * score_scale
        scores = jnp.where(valid_keys[:, None, None, :], scores, -1e+30)
        row_peak = lax.optimization_barrier(jnp.max(scores, axis=-1, keepdims=True))
        exp_scores = jnp.exp(scores - row_peak)
        attn_weights = exp_scores / lax.optimization_barrier(jnp.sum(exp_scores, axis=-1, keepdims=True))
        reduced_precision_weights = rounded(attn_weights)
        attn_out = rounded(jnp.einsum('bhqk,bkhd->bqhd', reduced_precision_weights, selected_values))
        grad_full = group_grad.astype(jnp.float32)
        row_delta = lax.optimization_barrier(jnp.sum(grad_full * attn_out, axis=-1))
        grad_weights = jnp.einsum('bqhd,bkhd->bhqk', grad_full, selected_values)
        score_gradient = rounded(attn_weights * (grad_weights - jnp.transpose(row_delta, (0, 2, 1))[..., None]))
        grad_query = rounded(jnp.einsum('bhqk,bkhd->bqhd', score_gradient, selected_keys) * score_scale)
        key_part = jnp.einsum('bhqk,bqhd->bkhd', score_gradient, query_full).reshape(per_group * NKB, BLOCK, col_count)
        value_part = jnp.einsum('bhqk,bqhd->bkhd', reduced_precision_weights, grad_full).reshape(per_group * NKB, BLOCK, col_count)
        flat_lists = group_lists.reshape(-1)
        key_accum = key_accum.at[flat_lists].add(key_part)
        value_accum = value_accum.at[flat_lists].add(value_part)
        return ((key_accum, value_accum), (attn_out, grad_query))
    inputs = (queries.reshape(N_SEQ, per_group, BLOCK, head_count, HD), d_attn.reshape(N_SEQ, per_group, BLOCK, head_count, HD), stored.reshape(N_SEQ, per_group, NKB), counts.reshape(N_SEQ, per_group))
    initial = (jnp.zeros((block_count, BLOCK, col_count), jnp.float32), jnp.zeros((block_count, BLOCK, col_count), jnp.float32))
    (key_accum, value_accum), (attn_all, grad_all) = lax.scan(one_group, initial, inputs)
    attn_low = attn_all.reshape(TOKENS, col_count).astype(jnp.bfloat16)
    d_query = grad_all.reshape(TOKENS, col_count).astype(jnp.bfloat16)
    d_key = (key_accum.reshape(TOKENS, col_count) * score_scale).astype(jnp.bfloat16)
    d_value = value_accum.reshape(TOKENS, col_count).astype(jnp.bfloat16)
    group_cols = HEAD_DEV * HD
    layer_sum = jnp.zeros((TOKENS, D), jnp.float32)
    for head_group in range(N_HEAD):
        col_start = head_group * group_cols
        partial_value = jnp.dot(attn_low[:, col_start:col_start + group_cols], out_weight[col_start:col_start + group_cols], preferred_element_type=jnp.float32)
        layer_sum = layer_sum + rounded(partial_value)
    layer_out = layer_sum.astype(jnp.bfloat16)
    weight_sum = jnp.zeros((col_count, D), jnp.float32)
    for seq_group in range(N_SEQ):
        row_start = seq_group * T_DEV
        partial_value = jnp.dot(attn_low[row_start:row_start + T_DEV].T, d_output[row_start:row_start + T_DEV], preferred_element_type=jnp.float32)
        weight_sum = weight_sum + rounded(partial_value)
    d_weight = weight_sum.astype(jnp.bfloat16)
    return (layer_out, d_query, d_key, d_value, d_weight)
```

```python
import functools
import math

import jax
import jax.numpy as jnp
from jax import lax
from jax.experimental import pallas as pl
from jax.experimental.pallas import tpu as pltpu
from jax.sharding import PartitionSpec as P

HD = 128
BLOCK = 128
FRAME_TOK = 384
PER_FRAME = FRAME_TOK // BLOCK
NZ = 4
NEG = -1e30
MESH = pl.DeviceIdType.MESH
VMEM = pl.BlockSpec(memory_space=pltpu.VMEM)
SMEM = pl.BlockSpec(memory_space=pltpu.SMEM)
ANY = pl.BlockSpec(memory_space=pl.ANY)
f32 = jnp.float32
bf16 = jnp.bfloat16
SWAPS = 8
S_K, S_V, S_Q, S_G, S_O, S_DQ, S_DK, S_DV = range(SWAPS)


def dot(a, b, ca, cb):
    return lax.dot_general(a, b, (((ca,), (cb,)), ((), ())), preferred_element_type=f32)


def store_kernel(n, *refs):
    sems = refs[2 * n]
    copies = [pltpu.make_async_copy(refs[i], refs[n + i], sems.at[i]) for i in range(n)]
    for c in copies:
        c.start()
    for c in copies:
        c.wait()


def store(arrays):
    n = len(arrays)
    return pl.pallas_call(
        functools.partial(store_kernel, n),
        out_shape=tuple(jax.ShapeDtypeStruct(a.shape, a.dtype) for a in arrays),
        in_specs=[VMEM] * n,
        out_specs=(ANY,) * n,
        scratch_shapes=[pltpu.SemaphoreType.DMA((n,))],
    )(*arrays)


def head(h):
    return slice(h * HD, (h + 1) * HD)


def place(nx):
    me, hd = lax.axis_index("seq"), lax.axis_index("head")
    z, x = me // nx, lax.rem(me, nx)
    xl, y, c = lax.rem(x, 2), hd // 2, lax.rem(hd, 2)
    e = x - xl + c
    return me, hd, z, x, xl, y, c, e


def mask_kernel(nx, keys_ref, count_ref, slot_ref, bias_ref):
    _, _, z, _, _, _, _, e = place(nx)
    frame = z * nx + e
    bias_ref[...] = jnp.full(bias_ref.shape, NEG, f32)
    logical = jnp.int32(0)
    for f in range(slot_ref.shape[0]):
        logical = jnp.where(slot_ref[f] == frame, jnp.int32(f), logical)
    for b in range(PER_FRAME):
        row = logical * PER_FRAME + b
        count = count_ref[row]

        @pl.loop(0, keys_ref.shape[1])
        def _(j):
            @pl.when(j < count)
            def _():
                entry = keys_ref[row, j]
                f = lax.div(entry, PER_FRAME)
                at = slice(b * BLOCK, (b + 1) * BLOCK)
                hit = lax.broadcasted_iota(jnp.int32, (PER_FRAME, BLOCK), 0) == entry - f * PER_FRAME
                bias_ref[slot_ref[f], :, at] = jnp.where(hit, 0.0, bias_ref[slot_ref[f], :, at])


def mask_bias(nx, block_keys, key_count, frame_slot, rows):
    return pl.pallas_call(
        functools.partial(mask_kernel, nx),
        out_shape=jax.ShapeDtypeStruct((frame_slot.shape[0], PER_FRAME, rows), f32),
        in_specs=[SMEM] * 3,
        out_specs=VMEM,
    )(block_keys, key_count, frame_slot)


def layer_kernel(
    nz, nx, nh,
    q_any, k_any, v_any, dout_any, ow_any, bias_ref,
    layer_ref, dq_ref, dk_ref, dv_ref, dw_ref,
    kv, qs, gs, os_ref, ot_ref, oo, ga, e_ref, g_all, ow, owt,
    ax, bx, cx, dqs, fin_ref, wp, wx, wb, wc, lp, lr, acc, acc_q, inv_ref, delta_ref,
    sw_s, sw_r, z2_s, z2_r, z1_s, z1_r, ec_s, ec_r,
    a_s, a_r, b_s, b_r, c_s, c_r, wx_s, wx_r, wb_s, wb_r, wc_s, wc_r, l_s, l_r,
    gy_s, gy_r, gc_s, gc_r, in_sem,
):
    me, hd, z, x, xl, y, c, e = place(nx)
    vme = z * nx + e
    same = xl == c
    other = jnp.logical_not(same)
    rows, width = q_any.shape
    heads = width // HD
    n_seq = nz * nx
    ny = nh // 2
    lw = layer_ref.shape[1]
    share = dw_ref.shape[1]
    scale = 1.0 / math.sqrt(HD)
    z1 = z + 1 - 2 * lax.rem(z, 2)
    z2 = lax.rem(z + 2, nz)
    z3 = lax.rem(z1 + 2, nz)
    zs = (z1, z3, z2, z)
    core = y * 2 + 1 - c
    mate = {"seq": vme, "head": y * 2 + xl}

    def dev(zz, ee):
        return {"seq": zz * nx + lax.div(ee, 2) * 2 + xl, "head": y * 2 + lax.rem(ee, 2)}

    def remote(src, dst, send, recv, device):
        return pltpu.make_async_remote_copy(
            src_ref=src, dst_ref=dst, send_sem=send, recv_sem=recv,
            device_id=device, device_id_type=MESH,
        )

    load_w = pltpu.make_async_copy(ow_any, ow, in_sem.at[0])
    load_g = pltpu.make_async_copy(dout_any, g_all.at[hd], in_sem.at[1])
    load_w.start()
    load_g.start()

    barrier = pltpu.get_barrier_semaphore()

    def greet(device):
        pl.semaphore_signal(barrier, inc=1, device_id=device, device_id_type=MESH)

    greet({"seq": z1 * nx + x})
    greet({"seq": z2 * nx + x})
    for dx in range(1, nx):
        greet({"seq": z * nx + lax.rem(x + dx, nx)})
    for dh in range(1, nh):
        greet({"head": lax.rem(hd + dh, nh)})

    for de in range(1, nx if nx > 2 else 1, 2):
        ee = lax.rem(e + de, nx)

        @pl.when(lax.div(ee, 2) != lax.div(e, 2))
        def _():
            greet(dev(z, ee))

    @pl.when(other)
    def _():
        greet(mate)

    peers = 2 + nx - 1 + nx // 2 - 1 + nh - 1
    pl.semaphore_wait(barrier, jnp.where(other, peers + 1, peers))

    def swap_refs(i, h, landed):
        at = slice(h * HD, (h + 1) * HD)
        slot = vme if landed else me
        return {
            S_K: lambda: (k_any.at[:, at], kv.at[h, slot, 0]),
            S_V: lambda: (v_any.at[:, at], kv.at[h, slot, 1]),
            S_Q: lambda: (q_any.at[:, at], qs.at[h]),
            S_G: lambda: (ga.at[:, at], gs.at[h]),
            S_O: lambda: (os_ref.at[h], oo.at[:, at]),
            S_DQ: lambda: (dqs.at[h], dq_ref.at[:, at]),
            S_DK: lambda: (fin_ref.at[h, 0], dk_ref.at[:, at]),
            S_DV: lambda: (fin_ref.at[h, 1], dv_ref.at[:, at]),
        }[i]()

    def swap_start(i, h):
        src, dst = swap_refs(i, h, False)

        @pl.when(same)
        def _():
            pltpu.make_async_copy(src, dst, sw_r.at[h, i]).start()

        @pl.when(other)
        def _():
            remote(src, dst, sw_s.at[h, i], sw_r.at[h, i], mate).start()

    def swap_wait(i, h):
        src, dst = swap_refs(i, h, True)

        @pl.when(same)
        def _():
            pltpu.make_async_copy(src, dst, sw_r.at[h, i]).wait()

        @pl.when(other)
        def _():
            remote(src, dst, sw_s.at[h, i], sw_r.at[h, i], mate).wait_recv()

    def swap_sent(i, h):
        src, dst = swap_refs(i, h, False)

        @pl.when(other)
        def _():
            remote(src, dst, sw_s.at[h, i], sw_r.at[h, i], mate).wait_send()

    def z2_copy(h, origin):
        block = kv.at[h, origin * nx + e]
        return remote(block, block, z2_s.at[h], z2_r.at[h], dev(z2, e))

    def z1_copy(h, i, origin):
        block = kv.at[h, origin * nx + e]
        return remote(block, block, z1_s.at[h, i], z1_r.at[h, i], dev(z1, e))

    def e_copy(h, k, de, source):
        block = kv.at[h, zs[k] * nx + source]
        return remote(
            block, block, ec_s.at[h, k, de - 1], ec_r.at[h, k, de - 1],
            dev(z, lax.rem(e + de, nx)),
        )

    def own(h):
        swap_wait(S_K, h)
        swap_wait(S_V, h)
        z2_copy(h, z).start()
        z1_copy(h, 0, z).start()
        for de in range(1, nx):
            e_copy(h, 3, de, e).start()

    def mid(h):
        z2_copy(h, z2).wait_recv()
        z1_copy(h, 1, z2).start()
        for de in range(1, nx):
            e_copy(h, 2, de, e).start()

    def fin(h):
        for i, origin in ((0, z1), (1, z3)):
            z1_copy(h, i, origin).wait_recv()
            for de in range(1, nx):
                e_copy(h, i, de, e).start()
        for k in (3, 2, 0, 1):
            for de in range(1, nx):
                e_copy(h, k, de, lax.rem(e - de + nx, nx)).wait_recv()

    def gather_sent(h):
        z2_copy(h, z).wait_send()
        z1_copy(h, 0, z).wait_send()
        z1_copy(h, 1, z2).wait_send()
        for k in range(nz):
            for de in range(1, nx):
                e_copy(h, k, de, e).wait_send()

    half = rows // 2

    def part_of(ref, p):
        return ref.at[pl.ds(p * half, half), :]

    def gy_copy(p, dy, landed):
        block = lax.rem(y - dy + ny, ny) * 2 + c if landed else hd
        return remote(
            part_of(dout_any, p), g_all.at[block, pl.ds(p * half, half), :],
            gy_s.at[p, dy - 1], gy_r.at[p, dy - 1],
            {"head": lax.rem(y + dy, ny) * 2 + c},
        )

    def gc_copy(p, dy, landed):
        block = lax.rem(y - dy + ny, ny) * 2 + (1 - c if landed else c)
        dst = g_all.at[block, pl.ds(p * half, half), :]
        src = dst if dy else part_of(dout_any, p)
        return remote(src, dst, gc_s.at[p, dy], gc_r.at[p, dy], {"head": core})

    def g_relay(p):
        for dy in range(1, ny):
            gy_copy(p, dy, True).wait_recv()
            gc_copy(p, dy, False).start()

    def forward(h):
        swap_wait(S_Q, h)
        q = qs[h]
        factor = math.log2(math.e) / math.sqrt(HD)

        def score_step(s, peak):
            t = dot(kv[h, s, 0], q, 1, 1).reshape(PER_FRAME, BLOCK, rows) * factor
            t = (t + bias_ref[s][:, None, :]).reshape(rows, rows)
            e_ref[s] = t
            return jnp.maximum(peak, jnp.max(t.reshape(rows // 8, 8, rows), axis=0))

        peak = lax.fori_loop(0, n_seq, score_step, jnp.full((8, rows), NEG, f32))
        peak = jnp.max(peak, axis=0, keepdims=True)

        def sum_step(s, carry):
            total, out = carry
            w = jnp.exp2(e_ref[s] - peak)
            e_ref[s] = w
            total = total + jnp.sum(w.reshape(rows // 8, 8, rows), axis=0)
            out = out + dot(kv[h, s, 1], w.astype(bf16), 0, 0)
            return total, out

        total, out = lax.fori_loop(
            0, n_seq, sum_step, (jnp.zeros((8, rows), f32), jnp.zeros((HD, rows), f32))
        )
        inv = 1.0 / jnp.sum(total, axis=0, keepdims=True)
        out = out * inv
        inv_ref[...] = jnp.broadcast_to(inv, (8, rows))
        ot_ref[...] = out.astype(bf16)
        os_ref[h] = out.T.astype(bf16)
        swap_start(S_O, h)

    def d_attention():
        for p in range(2):
            for dy in range(ny):
                gc_copy(p, dy, True).wait_recv()
        load_g.wait()
        load_w.wait()
        acc[...] = jnp.zeros_like(acc)

        @pl.loop(0, nh)
        def _(j):
            acc[...] += dot(g_all[j], ow[:, pl.ds(pl.multiple_of(j * lw, 128), lw)], 1, 1)

        ga[...] = acc[...].astype(bf16)
        for h in range(heads):
            swap_start(S_G, h)

    def frame(u):
        k = u // nx
        zz = lax.rem(jnp.where(k < 2, z1, z) + 2 * lax.rem((k + 1) // 2, 2), nz)
        de = lax.rem(lax.rem(u, nx) + 1, nx)
        return k, de, zz * nx + lax.rem(e + de, nx)

    def a_copy(h, k, de, s):
        return remote(
            kv.at[h, s], ax.at[h, k, de - 1], a_s.at[h, k, de - 1], a_r.at[h, k, de - 1],
            dev(z, lax.rem(e + de, nx)),
        )

    def a_slot(k, de):
        return zs[k] * nx + lax.rem(e + de, nx)

    def b_copy(h, k):
        return remote(
            kv.at[h, zs[k] * nx + e], bx.at[h, k], b_s.at[h, k], b_r.at[h, k], dev(z1, e)
        )

    def c_copy(h):
        return remote(kv.at[h, z2 * nx + e], cx.at[h], c_s.at[h], c_r.at[h], dev(z2, e))

    def backward(h):
        gather_sent(h)
        swap_wait(S_G, h)
        gt = gs[h].astype(f32).T
        delta = jnp.sum(gt * ot_ref[...].astype(f32), axis=0, keepdims=True)
        delta_ref[...] = jnp.broadcast_to(delta, (8, rows))
        acc_q[...] = jnp.zeros_like(acc_q)

        @pl.loop(0, n_seq)
        def _(u):
            k, de, s = frame(u)
            q, g = qs[h], gs[h]
            kb, vb = kv[h, s, 0], kv[h, s, 1]
            w = e_ref[s] * inv_ref[0:1, :]
            ds = (w * (dot(vb, g, 1, 1) - delta_ref[0:1, :])).astype(bf16)
            kv[h, s, 1] = dot(w.astype(bf16), g, 1, 0).astype(bf16)
            kv[h, s, 0] = dot(ds, q, 1, 0).astype(bf16)
            acc_q[...] += dot(kb, ds, 0, 0)

            @pl.when(de > 0)
            def _():
                a_copy(h, k, de, s).start()

        dqs[h] = (acc_q[...] * scale).T.astype(bf16)
        swap_start(S_DQ, h)

    def add_up(out, terms, factors=(1.0, 1.0)):
        for i in range(2):
            @pl.loop(0, rows // BLOCK)
            def _(r):
                at = pl.ds(pl.multiple_of(r * BLOCK, BLOCK), BLOCK)
                total = terms[0][i, at, :].astype(f32)
                for t in terms[1:]:
                    total += t[i, at, :].astype(f32)
                out[i, at, :] = (total * factors[i]).astype(bf16)

    def a_terms(h, k):
        for de in range(1, nx):
            a_copy(h, k, de, a_slot(k, de)).wait_recv()
        return [kv.at[h, zs[k] * nx + e]] + [ax.at[h, k, de - 1] for de in range(1, nx)]

    def rs_b(h):
        for k in (0, 1):
            terms = a_terms(h, k)
            add_up(terms[0], terms)
            b_copy(h, k).start()

    def rs_c(h):
        terms = a_terms(h, 2)
        b_copy(h, 1).wait_recv()
        add_up(terms[0], terms + [bx.at[h, 1]])
        c_copy(h).start()

    def rs_f(h):
        terms = a_terms(h, 3)
        b_copy(h, 0).wait_recv()
        c_copy(h).wait_recv()
        add_up(fin_ref.at[h], terms + [bx.at[h, 0], cx.at[h]], (scale, 1.0))
        swap_start(S_DK, h)
        swap_start(S_DV, h)

    def wx_copy(k, dx):
        px = lax.rem(x + dx, nx)
        return remote(
            wp.at[zs[k] * nx + px], wx.at[k, dx - 1], wx_s.at[k, dx - 1], wx_r.at[k, dx - 1],
            {"seq": z * nx + px},
        )

    def wb_copy(k):
        return remote(
            wp.at[zs[k] * nx + x], wb.at[k], wb_s.at[k], wb_r.at[k], {"seq": z1 * nx + x}
        )

    wc_copy = remote(wp.at[z2 * nx + x], wc, wc_s.at[0], wc_r.at[0], {"seq": z2 * nx + x})

    def w_parts():
        owt[...] = oo[...].astype(f32).T.astype(bf16)
        per = lw // share

        @pl.loop(0, nh)
        def _(j):
            if share % 128 == 0:
                for t in range(per):
                    wp[j * per + t] = jnp.dot(
                        owt[...], g_all[j, :, t * share:(t + 1) * share],
                        preferred_element_type=f32,
                    ).astype(bf16)
            else:
                r = jnp.dot(owt[...], g_all[j], preferred_element_type=f32).astype(bf16)
                for t in range(per):
                    wp[j * per + t] = r[:, t * share:(t + 1) * share]

        for k in range(nz):
            for dx in range(1, nx):
                wx_copy(k, dx).start()

    def w_add(out, k, extra):
        for dx in range(1, nx):
            wx_copy(k, dx).wait_recv()
        slot = zs[k] * nx + x

        @pl.loop(0, width // BLOCK)
        def _(r):
            at = pl.ds(pl.multiple_of(r * BLOCK, BLOCK), BLOCK)
            total = wp[slot, at, :].astype(f32)
            for dx in range(1, nx):
                total += wx[k, dx - 1, at, :].astype(f32)
            for t in extra:
                total += t[at, :].astype(f32)
            out[at, :] = total.astype(bf16)

    def w_b(k):
        w_add(wp.at[zs[k] * nx + x], k, [])
        wb_copy(k).start()

    def w_c():
        wb_copy(1).wait_recv()
        w_add(wp.at[z2 * nx + x], 2, [wb.at[1]])
        wc_copy.start()

    def w_f():
        wb_copy(0).wait_recv()
        wc_copy.wait_recv()
        w_add(dw_ref, 3, [wb.at[0], wc])

    def l_copy(dh):
        return remote(
            lp.at[dh], lr.at[dh - 1], l_s.at[dh - 1], l_r.at[dh - 1],
            {"head": lax.rem(hd + dh, nh)},
        )

    def layer_parts():
        @pl.loop(0, nh)
        def _(j):
            dh = lax.rem(j + 1, nh)
            at = pl.ds(pl.multiple_of(lax.rem(hd + dh, nh) * lw, 128), lw)
            lp[dh] = jnp.dot(oo[...], ow[:, at], preferred_element_type=f32).astype(bf16)

            @pl.when(dh > 0)
            def _():
                l_copy(dh).start()

    def layer_sum():
        @pl.loop(1, nh)
        def _(dh):
            l_copy(dh).wait_recv()

        @pl.loop(0, rows // BLOCK)
        def _(r):
            at = pl.ds(pl.multiple_of(r * BLOCK, BLOCK), BLOCK)
            total = lp[0, at, :].astype(f32)
            for dh in range(1, nh):
                total += lr[dh - 1, at, :].astype(f32)
            layer_ref[at, :] = total.astype(bf16)

    for h in range(heads):
        for i in (S_K, S_V, S_Q):
            swap_start(i, h)
    for p in range(2):
        for dy in range(1, ny):
            gy_copy(p, dy, False).start()
        gc_copy(p, 0, False).start()

    own(0)
    mid(0)
    own(1)
    g_relay(0)
    fin(0)
    forward(0)
    mid(1)
    own(2)
    g_relay(1)
    d_attention()
    backward(0)
    rs_b(0)
    mid(2)
    fin(1)
    forward(1)
    rs_c(0)
    backward(1)
    rs_b(1)
    fin(2)
    forward(2)
    rs_f(0)
    rs_c(1)
    for h in range(heads):
        swap_wait(S_O, h)
    w_parts()
    layer_parts()
    backward(2)
    rs_b(2)
    w_b(0)
    rs_f(1)
    w_b(1)
    rs_c(2)
    w_c()
    layer_sum()
    rs_f(2)
    w_f()

    for h in range(heads):
        for i in (S_DQ, S_DK, S_DV):
            swap_wait(i, h)
        for i in range(SWAPS):
            swap_sent(i, h)
        for k in range(nz):
            for de in range(1, nx):
                a_copy(h, k, de, a_slot(k, de)).wait_send()
        b_copy(h, 0).wait_send()
        b_copy(h, 1).wait_send()
        c_copy(h).wait_send()
    for p in range(2):
        for dy in range(1, ny):
            gy_copy(p, dy, False).wait_send()
        for dy in range(ny):
            gc_copy(p, dy, False).wait_send()
    for k in range(nz):
        for dx in range(1, nx):
            wx_copy(k, dx).wait_send()
    wb_copy(0).wait_send()
    wb_copy(1).wait_send()
    wc_copy.wait_send()
    for dh in range(1, nh):
        l_copy(dh).wait_send()


def layer(n_seq, nh, queries, keys, values, d_output, out_weight, bias):
    nz, nx = NZ, n_seq // NZ
    ny = nh // 2
    rows, width = queries.shape
    columns = out_weight.shape[1]
    heads, lw, share = width // HD, columns // nh, columns // n_seq
    dma = pltpu.SemaphoreType.DMA
    one = jax.ShapeDtypeStruct((rows, width), bf16)
    by_head = pltpu.VMEM((heads, rows, HD), bf16)
    flat = pltpu.VMEM((rows, width), bf16)
    pair = (2, rows, HD)
    sems = [
        (heads, SWAPS), (heads,), (heads, 2), (heads, nz, nx - 1),
        (heads, nz, nx - 1), (heads, 2), (heads,),
        (nz, nx - 1), (2,), (1,), (nh - 1,), (2, ny - 1), (2, ny),
    ]
    return pl.pallas_call(
        functools.partial(layer_kernel, nz, nx, nh),
        out_shape=(
            jax.ShapeDtypeStruct((rows, lw), bf16), one, one, one,
            jax.ShapeDtypeStruct((width, share), bf16),
        ),
        in_specs=[ANY] * 5 + [VMEM],
        out_specs=(VMEM,) * 5,
        scratch_shapes=[
            pltpu.VMEM((heads, n_seq) + pair, bf16),
            by_head,
            by_head,
            by_head,
            pltpu.VMEM((HD, rows), bf16),
            flat,
            flat,
            pltpu.VMEM((n_seq, rows, rows), f32),
            pltpu.VMEM((nh, rows, lw), bf16),
            pltpu.VMEM((width, columns), bf16),
            pltpu.VMEM((width, rows), bf16),
            pltpu.VMEM((heads, nz, nx - 1) + pair, bf16),
            pltpu.VMEM((heads, 2) + pair, bf16),
            pltpu.VMEM((heads,) + pair, bf16),
            by_head,
            pltpu.VMEM((heads,) + pair, bf16),
            pltpu.VMEM((n_seq, width, share), bf16),
            pltpu.VMEM((nz, nx - 1, width, share), bf16),
            pltpu.VMEM((2, width, share), bf16),
            pltpu.VMEM((width, share), bf16),
            pltpu.VMEM((nh, rows, lw), bf16),
            pltpu.VMEM((nh - 1, rows, lw), bf16),
            pltpu.VMEM((rows, width), f32),
            pltpu.VMEM((HD, rows), f32),
            pltpu.VMEM((8, rows), f32),
            pltpu.VMEM((8, rows), f32),
        ]
        + [dma(s) for s in sems for _ in range(2)]
        + [dma((2,))],
        compiler_params=pltpu.CompilerParams(
            collective_id=0, has_side_effects=True, vmem_limit_bytes=60 * 2**20
        ),
    )(queries, keys, values, d_output, out_weight, bias)


def on_device(
    n_seq, n_head,
    queries, keys, values, out_weight, d_output, block_keys, key_count, frame_slot,
):
    bias = mask_bias(n_seq // NZ, block_keys, key_count, frame_slot, queries.shape[0])
    return store(
        layer(n_seq, n_head, queries, keys, values, d_output, out_weight, bias)
    )


def solution(mesh):
    return jax.shard_map(
        functools.partial(on_device, mesh.shape["seq"], mesh.shape["head"]),
        mesh=mesh,
        in_specs=(
            P("seq", "head"),
            P("seq", "head"),
            P("seq", "head"),
            P("head", None),
            P("seq", "head"),
            P(),
            P(),
            P(),
        ),
        out_specs=(
            P("seq", "head"),
            P("seq", "head"),
            P("seq", "head"),
            P("seq", "head"),
            P("head", "seq"),
        ),
        check_vma=False,
    )
```

```python
import functools
import math

import jax
import jax.numpy as jnp
from jax import lax
from jax.experimental import pallas as pl
from jax.experimental.pallas import tpu as pltpu
from jax.sharding import PartitionSpec as P

HD = 128
BLOCK = 128
FRAME_TOK = 384
PER_FRAME = FRAME_TOK // BLOCK
NZ = 4
NEG = -1e30
MESH = pl.DeviceIdType.MESH
VMEM = pl.BlockSpec(memory_space=pltpu.VMEM)
SMEM = pl.BlockSpec(memory_space=pltpu.SMEM)
ANY = pl.BlockSpec(memory_space=pl.ANY)
f32 = jnp.float32
bf16 = jnp.bfloat16
KINDS = 9
T_K, T_V, T_Q, T_G, T_STAT, T_OUT, T_LSE, T_DQ, T_DKV = range(KINDS)


def dot(a, b, ca, cb):
    return lax.dot_general(a, b, (((ca,), (cb,)), ((), ())), preferred_element_type=f32)


def store_kernel(n, *refs):
    sems = refs[2 * n]
    copies = [pltpu.make_async_copy(refs[i], refs[n + i], sems.at[i]) for i in range(n)]
    for c in copies:
        c.start()
    for c in copies:
        c.wait()


def store(arrays):
    n = len(arrays)
    return pl.pallas_call(
        functools.partial(store_kernel, n),
        out_shape=tuple(jax.ShapeDtypeStruct(a.shape, a.dtype) for a in arrays),
        in_specs=[VMEM] * n,
        out_specs=(ANY,) * n,
        scratch_shapes=[pltpu.SemaphoreType.DMA((n,))],
    )(*arrays)


def head(h):
    return slice(h * HD, (h + 1) * HD)


def place(nx):
    me, hd = lax.axis_index("seq"), lax.axis_index("head")
    z, x = me // nx, lax.rem(me, nx)
    xl, y, c = lax.rem(x, 2), hd // 2, lax.rem(hd, 2)
    e = x - xl + c
    return me, hd, z, x, xl, y, c, e


def mask_kernel(nz, nx, keys_ref, count_ref, slot_ref, bias_ref):
    _, _, z, _, _, _, _, e = place(nx)
    rows = bias_ref.shape[2] // 2
    bias_ref[...] = jnp.full(bias_ref.shape, NEG, f32)
    for i, zz in enumerate((z, lax.rem(z + 2, nz))):
        frame = zz * nx + e
        logical = jnp.int32(0)
        for f in range(slot_ref.shape[0]):
            logical = jnp.where(slot_ref[f] == frame, jnp.int32(f), logical)
        for b in range(PER_FRAME):
            row = logical * PER_FRAME + b
            count = count_ref[row]
            at = slice(i * rows + b * BLOCK, i * rows + (b + 1) * BLOCK)

            @pl.loop(0, keys_ref.shape[1])
            def _(j):
                @pl.when(j < count)
                def _():
                    entry = keys_ref[row, j]
                    f = lax.div(entry, PER_FRAME)
                    sub = lax.broadcasted_iota(jnp.int32, (PER_FRAME, BLOCK), 0)
                    hit = sub == entry - f * PER_FRAME
                    slot = slot_ref[f]
                    bias_ref[slot, :, at] = jnp.where(hit, 0.0, bias_ref[slot, :, at])


def mask_bias(nx, block_keys, key_count, frame_slot, rows):
    return pl.pallas_call(
        functools.partial(mask_kernel, NZ, nx),
        out_shape=jax.ShapeDtypeStruct((frame_slot.shape[0], PER_FRAME, 2 * rows), f32),
        in_specs=[SMEM] * 3,
        out_specs=VMEM,
    )(block_keys, key_count, frame_slot)


def layer_kernel(
    nz, nx, nh,
    q_any, k_any, v_any, dout_any, ow_any, bias_ref,
    layer_ref, dq_ref, dk_ref, dv_ref, dw_ref,
    kv, qs, gs, os_ref, ls_ref, peak_ref, exps, stb, sto, opb, lsb, owt, oo, ga, gat,
    g_all, ow, ax, dqs, dqb, fin_ref, fb, wp, wx, wb, wc, lp, lr, acc, acc_q,
    t_s, t_r, z1_s, z1_r, ec_s, ec_r,
    a_s, a_r, wx_s, wx_r, wb_s, wb_r, wc_s, wc_r, l_s, l_r,
    gy_s, gy_r, gc_s, gc_r, in_sem,
):
    me, hd, z, x, xl, y, c, e = place(nx)
    same = xl == c
    other = jnp.logical_not(same)
    rows, width = q_any.shape
    heads = width // HD
    n_seq = nz * nx
    ny = nh // 2
    lw = layer_ref.shape[1]
    share = dw_ref.shape[1]
    scale = 1.0 / math.sqrt(HD)
    z1 = z + 1 - 2 * lax.rem(z, 2)
    z2 = lax.rem(z + 2, nz)
    z3 = lax.rem(z1 + 2, nz)
    zs = (z1, z3, z2, z)
    core = y * 2 + 1 - c

    def dev(zz, ee):
        return {"seq": zz * nx + lax.div(ee, 2) * 2 + xl, "head": y * 2 + lax.rem(ee, 2)}

    def remote(src, dst, send, recv, device):
        return pltpu.make_async_remote_copy(
            src_ref=src, dst_ref=dst, send_sem=send, recv_sem=recv,
            device_id=device, device_id_type=MESH,
        )

    load_w = pltpu.make_async_copy(ow_any, ow, in_sem.at[0])
    load_g = pltpu.make_async_copy(dout_any, g_all.at[hd], in_sem.at[1])
    load_w.start()
    load_g.start()

    barrier = pltpu.get_barrier_semaphore()

    def greet(device):
        pl.semaphore_signal(barrier, inc=1, device_id=device, device_id_type=MESH)

    greet({"seq": z1 * nx + x})
    greet({"seq": z2 * nx + x})
    for dx in range(1, nx):
        greet({"seq": z * nx + lax.rem(x + dx, nx)})
    for dh in range(1, nh):
        greet({"head": lax.rem(hd + dh, nh)})

    for de in range(1, nx if nx > 2 else 1, 2):
        ee = lax.rem(e + de, nx)

        @pl.when(lax.div(ee, 2) != lax.div(e, 2))
        def _():
            greet(dev(z, ee))

    @pl.when(other)
    def _():
        for zz in (z, z1, z2):
            greet({"seq": zz * nx + e, "head": y * 2 + xl})

    peers = 2 + nx - 1 + nx // 2 - 1 + nh - 1
    pl.semaphore_wait(barrier, jnp.where(other, peers + 3, peers))

    def move_refs(i, h, far, landed):
        at = slice(h * HD, (h + 1) * HD)
        part = slice(far * rows, (far + 1) * rows)
        slot = e if landed else x
        return {
            T_K: lambda: (k_any.at[:, at], kv.at[h, slot, 0]),
            T_V: lambda: (v_any.at[:, at], kv.at[h, slot, 1]),
            T_Q: lambda: (q_any.at[:, at], qs.at[h, part, :]),
            T_G: lambda: (ga.at[:, at], gs.at[h, part, :]),
            T_STAT: lambda: (sto.at[h], stb.at[h, far]),
            T_OUT: lambda: (os_ref.at[h, far], opb.at[h, far]),
            T_LSE: lambda: (ls_ref.at[h, far], lsb.at[h, far]),
            T_DQ: lambda: (dqs.at[h, far], dqb.at[h, far]),
            T_DKV: lambda: (fin_ref.at[h, far], fb.at[h, far]),
        }[i]()

    def move(i, h, far, landed, local, away):
        src, dst = move_refs(i, h, far, landed)
        zz = z if far == 0 else (z1 if i == T_DKV else z2)
        device = {"seq": zz * nx + e, "head": y * 2 + xl}
        send, recv = t_s.at[h, i, far], t_r.at[h, i, far]
        if far:
            away(remote(src, dst, send, recv, device))
            return

        @pl.when(other)
        def _():
            away(remote(src, dst, send, recv, device))

        if local is not None:
            @pl.when(same)
            def _():
                local(pltpu.make_async_copy(src, dst, recv))

    def fars(i):
        return (0,) if i in (T_K, T_V) else (0, 1)

    def move_start(i, h, far):
        move(i, h, far, False, lambda d: d.start(), lambda d: d.start())

    def move_wait(i, h, far):
        move(i, h, far, True, lambda d: d.wait(), lambda d: d.wait_recv())

    def move_sent(i, h, far):
        move(i, h, far, False, None, lambda d: d.wait_send())

    def z1_copy(h):
        return remote(
            kv.at[h, e], kv.at[h, nx + e], z1_s.at[h], z1_r.at[h], dev(z1, e)
        )

    def e_copy(h, k, de, source):
        block = kv.at[h, k * nx + source]
        return remote(
            block, block, ec_s.at[h, k, de - 1], ec_r.at[h, k, de - 1],
            dev(z, lax.rem(e + de, nx)),
        )

    def own(h):
        move_wait(T_K, h, 0)
        move_wait(T_V, h, 0)
        z1_copy(h).start()
        for de in range(1, nx):
            e_copy(h, 0, de, e).start()

    def fin(h):
        z1_copy(h).wait_recv()
        for de in range(1, nx):
            e_copy(h, 1, de, e).start()
        for k in range(2):
            for de in range(1, nx):
                e_copy(h, k, de, lax.rem(e - de + nx, nx)).wait_recv()

    def gather_sent(h):
        z1_copy(h).wait_send()
        for k in range(2):
            for de in range(1, nx):
                e_copy(h, k, de, e).wait_send()

    half = rows // 2

    def part_of(ref, p):
        return ref.at[pl.ds(p * half, half), :]

    def gy_copy(p, dy, landed):
        block = lax.rem(y - dy + ny, ny) * 2 + c if landed else hd
        return remote(
            part_of(dout_any, p), g_all.at[block, pl.ds(p * half, half), :],
            gy_s.at[p, dy - 1], gy_r.at[p, dy - 1],
            {"head": lax.rem(y + dy, ny) * 2 + c},
        )

    def gc_copy(p, dy, landed):
        block = lax.rem(y - dy + ny, ny) * 2 + (1 - c if landed else c)
        dst = g_all.at[block, pl.ds(p * half, half), :]
        src = dst if dy else part_of(dout_any, p)
        return remote(src, dst, gc_s.at[p, dy], gc_r.at[p, dy], {"head": core})

    def g_relay(p):
        for dy in range(1, ny):
            gy_copy(p, dy, True).wait_recv()
            gc_copy(p, dy, False).start()

    def slot_frame(s):
        return jnp.where(s < nx, z * nx + s, z1 * nx + s - nx)

    def forward(h):
        move_wait(T_Q, h, 0)
        move_wait(T_Q, h, 1)
        factor = math.log2(math.e) / math.sqrt(HD)
        cols = 2 * rows

        def step(s, carry):
            peak, total, out = carry
            t = dot(kv[h, s, 0], qs[h], 1, 1).reshape(PER_FRAME, BLOCK, cols) * factor
            t = (t + bias_ref[slot_frame(s)][:, None, :]).reshape(rows, cols)
            top = jnp.max(jnp.max(t.reshape(rows // 8, 8, cols), axis=0), axis=0, keepdims=True)
            new = jnp.maximum(peak, top)
            less = jnp.exp2(peak - new)
            w = jnp.exp2(t - new)
            low = w.astype(bf16)
            exps[h, s] = low
            peak_ref[h, s] = jnp.broadcast_to(new, (8, cols))
            total = total * less + jnp.sum(w.reshape(rows // 8, 8, cols), axis=0)
            out = out * less + dot(kv[h, s, 1], low, 0, 0)
            return new, total, out

        peak, total, out = lax.fori_loop(
            0, 2 * nx, step,
            (jnp.full((1, cols), NEG, f32), jnp.zeros((8, cols), f32), jnp.zeros((HD, cols), f32)),
        )
        total = jnp.sum(total, axis=0, keepdims=True)
        out = (out * (1.0 / total)).astype(bf16)
        lse = jnp.broadcast_to(peak + jnp.log2(total), (8, cols))
        for far in range(2):
            os_ref[h, far] = out[:, far * rows:(far + 1) * rows]
            ls_ref[h, far] = lse[:, far * rows:(far + 1) * rows]
            move_start(T_OUT, h, far)
            move_start(T_LSE, h, far)

    def combine(h):
        for far in range(2):
            move_wait(T_OUT, h, far)
            move_wait(T_LSE, h, far)
        one, two = lsb[h, 0, 0:1, :], lsb[h, 1, 0:1, :]
        top = jnp.maximum(one, two)
        lse = top + jnp.log2(jnp.exp2(one - top) + jnp.exp2(two - top))
        out = opb[h, 0].astype(f32) * jnp.exp2(one - lse) + opb[h, 1].astype(f32) * jnp.exp2(two - lse)
        low = out.astype(bf16)
        owt[head(h), :] = low
        oo[:, head(h)] = out.T.astype(bf16)
        delta = jnp.sum(
            gat[head(h), :].astype(f32) * low.astype(f32), axis=0, keepdims=True
        )
        sub = lax.broadcasted_iota(jnp.int32, (8, rows), 0)
        sto[h] = jnp.where(sub < 4, lse, delta)
        move_start(T_STAT, h, 0)
        move_start(T_STAT, h, 1)

    def d_attention():
        for p in range(2):
            for dy in range(ny):
                gc_copy(p, dy, True).wait_recv()
        load_g.wait()
        load_w.wait()
        acc[...] = jnp.zeros_like(acc)

        @pl.loop(0, nh)
        def _(j):
            acc[...] += dot(g_all[j], ow[:, pl.ds(pl.multiple_of(j * lw, 128), lw)], 1, 1)

        ga[...] = acc[...].astype(bf16)
        for h in range(heads):
            move_start(T_G, h, 0)
            move_start(T_G, h, 1)
        gat[...] = acc[...].T.astype(bf16)

    def a_copy(h, k, de, s):
        return remote(
            kv.at[h, s], ax.at[h, k, de - 1], a_s.at[h, k, de - 1], a_r.at[h, k, de - 1],
            dev(z, lax.rem(e + de, nx)),
        )

    def a_slot(k, de):
        return k * nx + lax.rem(e + de, nx)

    def backward(h):
        gather_sent(h)
        for far in range(2):
            move_wait(T_G, h, far)
            move_wait(T_STAT, h, far)
        lse = jnp.concatenate([stb[h, 0, 0:1, :], stb[h, 1, 0:1, :]], axis=1)
        delta = jnp.concatenate([stb[h, 0, 4:5, :], stb[h, 1, 4:5, :]], axis=1)
        acc_q[...] = jnp.zeros_like(acc_q)

        @pl.loop(0, 2 * nx)
        def _(u):
            k = 1 - u // nx
            de = lax.rem(lax.rem(u, nx) + 1, nx)
            s = k * nx + lax.rem(e + de, nx)
            q, g = qs[h], gs[h]
            kb, vb = kv[h, s, 0], kv[h, s, 1]
            w = exps[h, s].astype(f32) * jnp.exp2(peak_ref[h, s, 0:1, :] - lse)
            ds = (w * (dot(vb, g, 1, 1) - delta)).astype(bf16)
            kv[h, s, 1] = dot(w.astype(bf16), g, 1, 0).astype(bf16)
            kv[h, s, 0] = dot(ds, q, 1, 0).astype(bf16)
            acc_q[...] += dot(kb, ds, 0, 0)

            @pl.when(de > 0)
            def _():
                a_copy(h, k, de, s).start()

        for far in range(2):
            dqs[h, far] = acc_q[:, far * rows:(far + 1) * rows].T.astype(bf16)
            move_start(T_DQ, h, far)

    def add_up(out, terms, factor=1.0):
        @pl.loop(0, rows // BLOCK)
        def _(r):
            at = pl.ds(pl.multiple_of(r * BLOCK, BLOCK), BLOCK)
            total = terms[0][at, :].astype(f32)
            for t in terms[1:]:
                total += t[at, :].astype(f32)
            out[at, :] = (total * factor).astype(bf16)

    def keys_sum(h):
        for k in (1, 0):
            for de in range(1, nx):
                a_copy(h, k, de, a_slot(k, de)).wait_recv()
            for i in range(2):
                add_up(
                    fin_ref.at[h, k, i],
                    [kv.at[h, k * nx + e, i]] + [ax.at[h, k, de - 1, i] for de in range(1, nx)],
                )
            move_start(T_DKV, h, k)

    def finish(h):
        at = head(h)
        for far in range(2):
            move_wait(T_DQ, h, far)
        add_up(dq_ref.at[:, at], [dqb.at[h, 0], dqb.at[h, 1]], scale)
        for far in range(2):
            move_wait(T_DKV, h, far)
        add_up(dk_ref.at[:, at], [fb.at[h, 0, 0], fb.at[h, 1, 0]], scale)
        add_up(dv_ref.at[:, at], [fb.at[h, 0, 1], fb.at[h, 1, 1]])

    def wx_copy(k, dx):
        px = lax.rem(x + dx, nx)
        return remote(
            wp.at[zs[k] * nx + px], wx.at[k, dx - 1], wx_s.at[k, dx - 1], wx_r.at[k, dx - 1],
            {"seq": z * nx + px},
        )

    def wb_copy(k):
        return remote(
            wp.at[zs[k] * nx + x], wb.at[k], wb_s.at[k], wb_r.at[k], {"seq": z1 * nx + x}
        )

    wc_copy = remote(wp.at[z2 * nx + x], wc, wc_s.at[0], wc_r.at[0], {"seq": z2 * nx + x})

    def w_parts():
        per = lw // share

        @pl.loop(0, nh)
        def _(j):
            if share % 128 == 0:
                for t in range(per):
                    wp[j * per + t] = jnp.dot(
                        owt[...], g_all[j, :, t * share:(t + 1) * share],
                        preferred_element_type=f32,
                    ).astype(bf16)
            else:
                r = jnp.dot(owt[...], g_all[j], preferred_element_type=f32).astype(bf16)
                for t in range(per):
                    wp[j * per + t] = r[:, t * share:(t + 1) * share]

        for k in range(nz):
            for dx in range(1, nx):
                wx_copy(k, dx).start()

    def w_add(out, k, extra):
        for dx in range(1, nx):
            wx_copy(k, dx).wait_recv()
        slot = zs[k] * nx + x

        @pl.loop(0, width // BLOCK)
        def _(r):
            at = pl.ds(pl.multiple_of(r * BLOCK, BLOCK), BLOCK)
            total = wp[slot, at, :].astype(f32)
            for dx in range(1, nx):
                total += wx[k, dx - 1, at, :].astype(f32)
            for t in extra:
                total += t[at, :].astype(f32)
            out[at, :] = total.astype(bf16)

    def w_b(k):
        w_add(wp.at[zs[k] * nx + x], k, [])
        wb_copy(k).start()

    def w_c():
        wb_copy(1).wait_recv()
        w_add(wp.at[z2 * nx + x], 2, [wb.at[1]])
        wc_copy.start()

    def w_f():
        wb_copy(0).wait_recv()
        wc_copy.wait_recv()
        w_add(dw_ref, 3, [wb.at[0], wc])

    def l_copy(dh):
        return remote(
            lp.at[dh], lr.at[dh - 1], l_s.at[dh - 1], l_r.at[dh - 1],
            {"head": lax.rem(hd + dh, nh)},
        )

    def layer_parts():
        @pl.loop(0, nh)
        def _(j):
            dh = lax.rem(j + 1, nh)
            at = pl.ds(pl.multiple_of(lax.rem(hd + dh, nh) * lw, 128), lw)
            lp[dh] = jnp.dot(oo[...], ow[:, at], preferred_element_type=f32).astype(bf16)

            @pl.when(dh > 0)
            def _():
                l_copy(dh).start()

    def layer_sum():
        @pl.loop(1, nh)
        def _(dh):
            l_copy(dh).wait_recv()

        @pl.loop(0, rows // BLOCK)
        def _(r):
            at = pl.ds(pl.multiple_of(r * BLOCK, BLOCK), BLOCK)
            total = lp[0, at, :].astype(f32)
            for dh in range(1, nh):
                total += lr[dh - 1, at, :].astype(f32)
            layer_ref[at, :] = total.astype(bf16)

    for h in range(heads):
        for i in (T_K, T_V, T_Q):
            for far in fars(i):
                move_start(i, h, far)
    for p in range(2):
        for dy in range(1, ny):
            gy_copy(p, dy, False).start()
        gc_copy(p, 0, False).start()

    own(0)
    own(1)
    own(2)
    fin(0)
    forward(0)
    g_relay(0)
    fin(1)
    forward(1)
    g_relay(1)
    d_attention()
    combine(0)
    fin(2)
    forward(2)
    combine(1)
    backward(0)
    combine(2)
    w_parts()
    layer_parts()
    keys_sum(0)
    backward(1)
    keys_sum(1)
    w_b(0)
    backward(2)
    keys_sum(2)
    w_b(1)
    finish(0)
    w_c()
    finish(1)
    layer_sum()
    finish(2)
    w_f()

    for h in range(heads):
        for i in range(KINDS):
            for far in fars(i):
                move_sent(i, h, far)
        for k in range(2):
            for de in range(1, nx):
                a_copy(h, k, de, a_slot(k, de)).wait_send()
    for p in range(2):
        for dy in range(1, ny):
            gy_copy(p, dy, False).wait_send()
        for dy in range(ny):
            gc_copy(p, dy, False).wait_send()
    for k in range(nz):
        for dx in range(1, nx):
            wx_copy(k, dx).wait_send()
    wb_copy(0).wait_send()
    wb_copy(1).wait_send()
    wc_copy.wait_send()
    for dh in range(1, nh):
        l_copy(dh).wait_send()


def layer(n_seq, nh, queries, keys, values, d_output, out_weight, bias):
    nz, nx = NZ, n_seq // NZ
    ny = nh // 2
    rows, width = queries.shape
    columns = out_weight.shape[1]
    heads, lw, share = width // HD, columns // nh, columns // n_seq
    dma = pltpu.SemaphoreType.DMA
    one = jax.ShapeDtypeStruct((rows, width), bf16)
    flat = pltpu.VMEM((rows, width), bf16)
    pair = (2, rows, HD)
    sems = [
        (heads, KINDS, 2), (heads,), (heads, 2, nx - 1),
        (heads, 2, nx - 1),
        (nz, nx - 1), (2,), (1,), (nh - 1,), (2, ny - 1), (2, ny),
    ]
    return pl.pallas_call(
        functools.partial(layer_kernel, nz, nx, nh),
        out_shape=(
            jax.ShapeDtypeStruct((rows, lw), bf16), one, one, one,
            jax.ShapeDtypeStruct((width, share), bf16),
        ),
        in_specs=[ANY] * 5 + [VMEM],
        out_specs=(VMEM,) * 5,
        scratch_shapes=[
            pltpu.VMEM((heads, 2 * nx) + pair, bf16),
            pltpu.VMEM((heads, 2 * rows, HD), bf16),
            pltpu.VMEM((heads, 2 * rows, HD), bf16),
            pltpu.VMEM((heads, 2, HD, rows), bf16),
            pltpu.VMEM((heads, 2, 8, rows), f32),
            pltpu.VMEM((heads, 2 * nx, 8, 2 * rows), f32),
            pltpu.VMEM((heads, 2 * nx, rows, 2 * rows), bf16),
            pltpu.VMEM((heads, 2, 8, rows), f32),
            pltpu.VMEM((heads, 8, rows), f32),
            pltpu.VMEM((heads, 2, HD, rows), bf16),
            pltpu.VMEM((heads, 2, 8, rows), f32),
            pltpu.VMEM((width, rows), bf16),
            flat,
            flat,
            pltpu.VMEM((width, rows), bf16),
            pltpu.VMEM((nh, rows, lw), bf16),
            pltpu.VMEM((width, columns), bf16),
            pltpu.VMEM((heads, 2, nx - 1) + pair, bf16),
            pltpu.VMEM((heads,) + pair, bf16),
            pltpu.VMEM((heads,) + pair, bf16),
            pltpu.VMEM((heads, 2) + pair, bf16),
            pltpu.VMEM((heads, 2) + pair, bf16),
            pltpu.VMEM((n_seq, width, share), bf16),
            pltpu.VMEM((nz, nx - 1, width, share), bf16),
            pltpu.VMEM((2, width, share), bf16),
            pltpu.VMEM((width, share), bf16),
            pltpu.VMEM((nh, rows, lw), bf16),
            pltpu.VMEM((nh - 1, rows, lw), bf16),
            pltpu.VMEM((rows, width), f32),
            pltpu.VMEM((HD, 2 * rows), f32),
        ]
        + [dma(s) for s in sems for _ in range(2)]
        + [dma((2,))],
        compiler_params=pltpu.CompilerParams(
            collective_id=0, has_side_effects=True, vmem_limit_bytes=60 * 2**20
        ),
    )(queries, keys, values, d_output, out_weight, bias)


def on_device(
    n_seq, n_head,
    queries, keys, values, out_weight, d_output, block_keys, key_count, frame_slot,
):
    bias = mask_bias(n_seq // NZ, block_keys, key_count, frame_slot, queries.shape[0])
    return store(
        layer(n_seq, n_head, queries, keys, values, d_output, out_weight, bias)
    )


def solution(mesh):
    return jax.shard_map(
        functools.partial(on_device, mesh.shape["seq"], mesh.shape["head"]),
        mesh=mesh,
        in_specs=(
            P("seq", "head"),
            P("seq", "head"),
            P("seq", "head"),
            P("head", None),
            P("seq", "head"),
            P(),
            P(),
            P(),
        ),
        out_specs=(
            P("seq", "head"),
            P("seq", "head"),
            P("seq", "head"),
            P("seq", "head"),
            P("head", "seq"),
        ),
        check_vma=False,
    )
```

```python
import functools
import math

import jax
import jax.numpy as jnp
from jax import lax
from jax.experimental import pallas as pl
from jax.experimental.pallas import tpu as pltpu
from jax.sharding import PartitionSpec as P

HD = 128
BLOCK = 128
FRAME_TOK = 384
PER_FRAME = FRAME_TOK // BLOCK
NZ = 4
NEG = -1e30
MESH = pl.DeviceIdType.MESH
VMEM = pl.BlockSpec(memory_space=pltpu.VMEM)
SMEM = pl.BlockSpec(memory_space=pltpu.SMEM)
ANY = pl.BlockSpec(memory_space=pl.ANY)
f32 = jnp.float32
bf16 = jnp.bfloat16
KINDS = 9
T_K, T_V, T_Q, T_G, T_STAT, T_OUT, T_LSE, T_DQ, T_DKV = range(KINDS)


def dot(a, b, ca, cb):
    return lax.dot_general(a, b, (((ca,), (cb,)), ((), ())), preferred_element_type=f32)


def store_kernel(n, *refs):
    sems = refs[2 * n]
    copies = [pltpu.make_async_copy(refs[i], refs[n + i], sems.at[i]) for i in range(n)]
    for c in copies:
        c.start()
    for c in copies:
        c.wait()


def store(arrays):
    n = len(arrays)
    return pl.pallas_call(
        functools.partial(store_kernel, n),
        out_shape=tuple(jax.ShapeDtypeStruct(a.shape, a.dtype) for a in arrays),
        in_specs=[VMEM] * n,
        out_specs=(ANY,) * n,
        scratch_shapes=[pltpu.SemaphoreType.DMA((n,))],
    )(*arrays)


def head(h):
    return slice(h * HD, (h + 1) * HD)


def place(nx):
    me, hd = lax.axis_index("seq"), lax.axis_index("head")
    z, x = me // nx, lax.rem(me, nx)
    xl, y, c = lax.rem(x, 2), hd // 2, lax.rem(hd, 2)
    e = x - xl + c
    return me, hd, z, x, xl, y, c, e


def layer_kernel(
    nz, nx, nh,
    q_any, k_any, v_any, dout_any, ow_any, keys_ref, count_ref, slot_ref,
    layer_ref, dq_ref, dk_ref, dv_ref, dw_ref,
    kv, qs, gs, os_ref, ls_ref, peak_ref, exps, stb, sto, opb, lsb, owt, oo, ga, gat,
    g_all, ow, ax, dqs, dqb, fin_ref, fb, wp, wx, wb, wc, wl, oall, g2, owtx, bias_ref, acc, acc_q,
    t_s, t_r, z1_s, z1_r, ec_s, ec_r,
    a_s, a_r, wx_s, wx_r, wb_s, wb_r, wc_s, wc_r, l_s, l_r,
    gy_s, gy_r, gc_s, gc_r, o_s, o_r, g2x_s, g2x_r, g2y_s, g2y_r, g2c_s, g2c_r, ox_s, ox_r, in_sem,
):
    me, hd, z, x, xl, y, c, e = place(nx)
    same = xl == c
    other = jnp.logical_not(same)
    rows, width = q_any.shape
    heads = width // HD
    n_seq = nz * nx
    ny = nh // 2
    lw = layer_ref.shape[1]
    share = dw_ref.shape[1]
    paired = nx == 2
    scale = 1.0 / math.sqrt(HD)
    z1 = z + 1 - 2 * lax.rem(z, 2)
    z2 = lax.rem(z + 2, nz)
    z3 = lax.rem(z1 + 2, nz)
    zs = (z1, z3, z2, z)
    core = y * 2 + 1 - c

    def dev(zz, ee):
        return {"seq": zz * nx + lax.div(ee, 2) * 2 + xl, "head": y * 2 + lax.rem(ee, 2)}

    def remote(src, dst, send, recv, device):
        return pltpu.make_async_remote_copy(
            src_ref=src, dst_ref=dst, send_sem=send, recv_sem=recv,
            device_id=device, device_id_type=MESH,
        )

    load_w = pltpu.make_async_copy(ow_any, ow, in_sem.at[0])
    load_g = pltpu.make_async_copy(dout_any, g_all.at[hd], in_sem.at[1])
    load_w.start()
    load_g.start()

    barrier = pltpu.get_barrier_semaphore()

    def greet(device):
        pl.semaphore_signal(barrier, inc=1, device_id=device, device_id_type=MESH)

    greet({"seq": z1 * nx + x})
    greet({"seq": z2 * nx + x})
    for dx in range(1, nx):
        greet({"seq": z * nx + lax.rem(x + dx, nx)})
    for dh in range(1, nh):
        greet({"head": lax.rem(hd + dh, nh)})

    for de in range(1, nx if nx > 2 else 1, 2):
        ee = lax.rem(e + de, nx)

        @pl.when(lax.div(ee, 2) != lax.div(e, 2))
        def _():
            greet(dev(z, ee))

    @pl.when(other)
    def _():
        for zz in (z, z1, z2):
            greet({"seq": zz * nx + e, "head": y * 2 + xl})

    peers = 2 + nx - 1 + nx // 2 - 1 + nh - 1
    pl.semaphore_wait(barrier, jnp.where(other, peers + 3, peers))

    def move_refs(i, h, far, landed):
        at = slice(h * HD, (h + 1) * HD)
        part = slice(far * rows, (far + 1) * rows)
        slot = e if landed else x
        return {
            T_K: lambda: (k_any.at[:, at], kv.at[h, slot, 0]),
            T_V: lambda: (v_any.at[:, at], kv.at[h, slot, 1]),
            T_Q: lambda: (q_any.at[:, at], qs.at[h, part, :]),
            T_G: lambda: (ga.at[:, at], gs.at[h, part, :]),
            T_STAT: lambda: (sto.at[h], stb.at[h, far]),
            T_OUT: lambda: (os_ref.at[h, far], opb.at[h, far]),
            T_LSE: lambda: (ls_ref.at[h, far], lsb.at[h, far]),
            T_DQ: lambda: (dqs.at[h, far], dqb.at[h, far]),
            T_DKV: lambda: (fin_ref.at[h, far], fb.at[h, far]),
        }[i]()

    def move(i, h, far, landed, local, away):
        src, dst = move_refs(i, h, far, landed)
        zz = z if far == 0 else (z1 if i == T_DKV else z2)
        device = {"seq": zz * nx + e, "head": y * 2 + xl}
        send, recv = t_s.at[h, i, far], t_r.at[h, i, far]
        if far:
            away(remote(src, dst, send, recv, device))
            return

        @pl.when(other)
        def _():
            away(remote(src, dst, send, recv, device))

        if local is not None:
            @pl.when(same)
            def _():
                local(pltpu.make_async_copy(src, dst, recv))

    def fars(i):
        return (0,) if i in (T_K, T_V) else (0, 1)

    def move_start(i, h, far):
        move(i, h, far, False, lambda d: d.start(), lambda d: d.start())

    def move_wait(i, h, far):
        move(i, h, far, True, lambda d: d.wait(), lambda d: d.wait_recv())

    def move_sent(i, h, far):
        move(i, h, far, False, None, lambda d: d.wait_send())

    def z1_copy(h):
        return remote(
            kv.at[h, e], kv.at[h, nx + e], z1_s.at[h], z1_r.at[h], dev(z1, e)
        )

    def e_copy(h, k, de, source):
        block = kv.at[h, k * nx + source]
        return remote(
            block, block, ec_s.at[h, k, de - 1], ec_r.at[h, k, de - 1],
            dev(z, lax.rem(e + de, nx)),
        )

    def own(h):
        move_wait(T_K, h, 0)
        move_wait(T_V, h, 0)
        z1_copy(h).start()
        for de in range(1, nx):
            e_copy(h, 0, de, e).start()

    def fin(h):
        z1_copy(h).wait_recv()
        for de in range(1, nx):
            e_copy(h, 1, de, e).start()
        for k in range(2):
            for de in range(1, nx):
                e_copy(h, k, de, lax.rem(e - de + nx, nx)).wait_recv()

    def gather_sent(h):
        z1_copy(h).wait_send()
        for k in range(2):
            for de in range(1, nx):
                e_copy(h, k, de, e).wait_send()

    half = rows // 2

    def part_of(ref, p):
        return ref.at[pl.ds(p * half, half), :]

    def gy_copy(p, dy, landed):
        block = lax.rem(y - dy + ny, ny) * 2 + c if landed else hd
        return remote(
            part_of(dout_any, p), g_all.at[block, pl.ds(p * half, half), :],
            gy_s.at[p, dy - 1], gy_r.at[p, dy - 1],
            {"head": lax.rem(y + dy, ny) * 2 + c},
        )

    def gc_copy(p, dy, landed):
        block = lax.rem(y - dy + ny, ny) * 2 + (1 - c if landed else c)
        dst = g_all.at[block, pl.ds(p * half, half), :]
        src = dst if dy else part_of(dout_any, p)
        return remote(src, dst, gc_s.at[p, dy], gc_r.at[p, dy], {"head": core})

    def g_relay(p):
        for dy in range(1, ny):
            gy_copy(p, dy, True).wait_recv()
            gc_copy(p, dy, False).start()

    def build_mask():
        shape = (n_seq, PER_FRAME, BLOCK)
        ids = lax.broadcasted_iota(jnp.int32, shape, 0) * PER_FRAME + lax.broadcasted_iota(
            jnp.int32, shape, 1
        )
        for i, zz in enumerate((z, z2)):
            logical = jnp.int32(0)
            for f in range(n_seq):
                logical = jnp.where(slot_ref[f] == zz * nx + e, jnp.int32(f), logical)
            for b in range(PER_FRAME):
                row = logical * PER_FRAME + b
                count = count_ref[row]

                def entry_step(j, bias):
                    entry = keys_ref[row, j]
                    f = lax.div(entry, PER_FRAME)
                    stored = slot_ref[f] * PER_FRAME + entry - f * PER_FRAME
                    return jnp.where(ids == jnp.where(j < count, stored, -1), 0.0, bias)

                at = slice(i * rows + b * BLOCK, i * rows + (b + 1) * BLOCK)
                bias_ref[:, :, at] = lax.fori_loop(
                    0, keys_ref.shape[1], entry_step, jnp.full(shape, NEG, f32)
                )

    def slot_frame(s):
        return jnp.where(s < nx, z * nx + s, z1 * nx + s - nx)

    def forward(h):
        move_wait(T_Q, h, 0)
        move_wait(T_Q, h, 1)
        factor = math.log2(math.e) / math.sqrt(HD)
        cols = 2 * rows

        def step(s, carry):
            peak, total, out = carry
            t = dot(kv[h, s, 0], qs[h], 1, 1).reshape(PER_FRAME, BLOCK, cols) * factor
            t = (t + bias_ref[slot_frame(s)][:, None, :]).reshape(rows, cols)
            top = jnp.max(jnp.max(t.reshape(rows // 8, 8, cols), axis=0), axis=0, keepdims=True)
            new = jnp.maximum(peak, top)
            less = jnp.exp2(peak - new)
            w = jnp.exp2(t - new)
            low = w.astype(bf16)
            exps[h, s] = low
            peak_ref[h, s] = jnp.broadcast_to(new, (8, cols))
            total = total * less + jnp.sum(w.reshape(rows // 8, 8, cols), axis=0)
            out = out * less + dot(kv[h, s, 1], low, 0, 0)
            return new, total, out

        peak, total, out = lax.fori_loop(
            0, 2 * nx, step,
            (jnp.full((1, cols), NEG, f32), jnp.zeros((8, cols), f32), jnp.zeros((HD, cols), f32)),
        )
        total = jnp.sum(total, axis=0, keepdims=True)
        out = (out * (1.0 / total)).astype(bf16)
        lse = jnp.broadcast_to(peak + jnp.log2(total), (8, cols))
        for far in range(2):
            os_ref[h, far] = out[:, far * rows:(far + 1) * rows]
            ls_ref[h, far] = lse[:, far * rows:(far + 1) * rows]
            move_start(T_OUT, h, far)
            move_start(T_LSE, h, far)

    def combine(h):
        for far in range(2):
            move_wait(T_OUT, h, far)
            move_wait(T_LSE, h, far)
        one, two = lsb[h, 0, 0:1, :], lsb[h, 1, 0:1, :]
        top = jnp.maximum(one, two)
        lse = top + jnp.log2(jnp.exp2(one - top) + jnp.exp2(two - top))
        out = opb[h, 0].astype(f32) * jnp.exp2(one - lse) + opb[h, 1].astype(f32) * jnp.exp2(two - lse)
        low = out.astype(bf16)
        owt[head(h), :] = low
        oo[:, head(h)] = out.T.astype(bf16)
        delta = jnp.sum(
            gat[head(h), :].astype(f32) * low.astype(f32), axis=0, keepdims=True
        )
        sub = lax.broadcasted_iota(jnp.int32, (8, rows), 0)
        sto[h] = jnp.where(sub < 4, lse, delta)
        move_start(T_STAT, h, 0)
        move_start(T_STAT, h, 1)
        if paired:
            ox_copy(h).start()
        for dh in range(1, nh):
            o_copy(h, dh).start()

    def d_attention():
        for p in range(2):
            for dy in range(ny):
                gc_copy(p, dy, True).wait_recv()
        load_g.wait()
        load_w.wait()
        acc[...] = jnp.zeros_like(acc)

        @pl.loop(0, nh)
        def _(j):
            acc[...] += dot(g_all[j], ow[:, pl.ds(pl.multiple_of(j * lw, 128), lw)], 1, 1)

        ga[...] = acc[...].astype(bf16)
        for h in range(heads):
            move_start(T_G, h, 0)
            move_start(T_G, h, 1)
        gat[...] = acc[...].T.astype(bf16)

    def a_copy(h, k, de, s):
        return remote(
            kv.at[h, s], ax.at[h, k, de - 1], a_s.at[h, k, de - 1], a_r.at[h, k, de - 1],
            dev(z, lax.rem(e + de, nx)),
        )

    def a_slot(k, de):
        return k * nx + lax.rem(e + de, nx)

    def backward(h):
        gather_sent(h)
        for far in range(2):
            move_wait(T_G, h, far)
            move_wait(T_STAT, h, far)
        lse = jnp.concatenate([stb[h, 0, 0:1, :], stb[h, 1, 0:1, :]], axis=1)
        delta = jnp.concatenate([stb[h, 0, 4:5, :], stb[h, 1, 4:5, :]], axis=1)
        acc_q[...] = jnp.zeros_like(acc_q)

        @pl.loop(0, 2 * nx)
        def _(u):
            k = 1 - u // nx
            de = lax.rem(lax.rem(u, nx) + 1, nx)
            s = k * nx + lax.rem(e + de, nx)
            q, g = qs[h], gs[h]
            kb, vb = kv[h, s, 0], kv[h, s, 1]
            w = exps[h, s].astype(f32) * jnp.exp2(peak_ref[h, s, 0:1, :] - lse)
            ds = (w * (dot(vb, g, 1, 1) - delta)).astype(bf16)
            kv[h, s, 1] = dot(w.astype(bf16), g, 1, 0).astype(bf16)
            kv[h, s, 0] = dot(ds, q, 1, 0).astype(bf16)
            acc_q[...] += dot(kb, ds, 0, 0)

            @pl.when(de > 0)
            def _():
                a_copy(h, k, de, s).start()

        for far in range(2):
            dqs[h, far] = acc_q[:, far * rows:(far + 1) * rows].T.astype(bf16)
            move_start(T_DQ, h, far)

    def add_up(out, terms, factor=1.0):
        @pl.loop(0, rows // BLOCK)
        def _(r):
            at = pl.ds(pl.multiple_of(r * BLOCK, BLOCK), BLOCK)
            total = terms[0][at, :].astype(f32)
            for t in terms[1:]:
                total += t[at, :].astype(f32)
            out[at, :] = (total * factor).astype(bf16)

    def keys_sum(h):
        for k in (1, 0):
            for de in range(1, nx):
                a_copy(h, k, de, a_slot(k, de)).wait_recv()
            for i in range(2):
                add_up(
                    fin_ref.at[h, k, i],
                    [kv.at[h, k * nx + e, i]] + [ax.at[h, k, de - 1, i] for de in range(1, nx)],
                )
            move_start(T_DKV, h, k)

    def finish(h):
        at = head(h)
        for far in range(2):
            move_wait(T_DQ, h, far)
        add_up(dq_ref.at[:, at], [dqb.at[h, 0], dqb.at[h, 1]], scale)
        for far in range(2):
            move_wait(T_DKV, h, far)
        add_up(dk_ref.at[:, at], [fb.at[h, 0, 0], fb.at[h, 1, 0]], scale)
        add_up(dv_ref.at[:, at], [fb.at[h, 0, 1], fb.at[h, 1, 1]])

    def ox_copy(h):
        return remote(
            owt.at[head(h), :], owtx.at[head(h), :], ox_s.at[h], ox_r.at[h],
            {"seq": z * nx + nx - 1 - x},
        )

    def g2x_copy():
        px = nx - 1 - x
        at = pl.ds(pl.multiple_of(px * share, 128), share)
        return remote(
            dout_any.at[:, at], g2.at[hd], g2x_s.at[0], g2x_r.at[0], {"seq": z * nx + px}
        )

    def g2y_copy(dy, landed):
        block = lax.rem(y - dy + ny, ny) * 2 + c if landed else hd
        return remote(
            g2.at[block], g2.at[block], g2y_s.at[dy - 1], g2y_r.at[dy - 1],
            {"head": lax.rem(y + dy, ny) * 2 + c},
        )

    def g2c_copy(dy, landed):
        block = g2.at[lax.rem(y - dy + ny, ny) * 2 + (1 - c if landed else c)]
        return remote(block, block, g2c_s.at[dy], g2c_r.at[dy], {"head": core})

    def g2_turn():
        g2x_copy().wait_recv()
        for dy in range(1, ny):
            g2y_copy(dy, False).start()
        g2c_copy(0, False).start()

    def g2_relay():
        for dy in range(1, ny):
            g2y_copy(dy, True).wait_recv()
            g2c_copy(dy, False).start()

    def wx_copy(k, dx):
        px = lax.rem(x + dx, nx)
        return remote(
            wp.at[zs[k] * nx + px], wx.at[k, dx - 1], wx_s.at[k, dx - 1], wx_r.at[k, dx - 1],
            {"seq": z * nx + px},
        )

    def w_slot(k):
        return k if paired else zs[k] * nx + x

    def wb_copy(k):
        return remote(
            wp.at[w_slot(k)], wb.at[k], wb_s.at[k], wb_r.at[k], {"seq": z1 * nx + x}
        )

    wc_copy = remote(wp.at[w_slot(2)], wc, wc_s.at[0], wc_r.at[0], {"seq": z2 * nx + x})
    per = lw // share

    def w_pair(k):
        p = zs[k] * nx + x
        at = pl.ds(pl.multiple_of(lax.rem(p, per) * share, 128), share)
        block = lax.div(p, per)
        wp[k] = (
            jnp.dot(owt[...], g_all[block, :, at], preferred_element_type=f32)
            + jnp.dot(owtx[...], g2[block], preferred_element_type=f32)
        ).astype(bf16)

    def w_parts():
        if paired:
            for dy in range(ny):
                g2c_copy(dy, True).wait_recv()
            for h in range(heads):
                ox_copy(h).wait_recv()
            for k in (1, 0):
                w_pair(k)
                wb_copy(k).start()
            for k in (2, 3):
                w_pair(k)
            return

        @pl.loop(0, nh)
        def _(j):
            r = jnp.dot(owt[...], g_all[j], preferred_element_type=f32).astype(bf16)
            for t in range(per):
                wp[j * per + t] = r[:, t * share:(t + 1) * share]

        for k in range(nz):
            for dx in range(1, nx):
                wx_copy(k, dx).start()

    def w_add(out, k, extra):
        slot = w_slot(k)
        if not paired:
            for dx in range(1, nx):
                wx_copy(k, dx).wait_recv()

        @pl.loop(0, width // BLOCK)
        def _(r):
            at = pl.ds(pl.multiple_of(r * BLOCK, BLOCK), BLOCK)
            total = wp[slot, at, :].astype(f32)
            if not paired:
                for dx in range(1, nx):
                    total += wx[k, dx - 1, at, :].astype(f32)
            for t in extra:
                total += t[at, :].astype(f32)
            out[at, :] = total.astype(bf16)

    def w_b(k):
        if not paired:
            w_add(wp.at[w_slot(k)], k, [])
            wb_copy(k).start()

    def w_c():
        wb_copy(1).wait_recv()
        w_add(wp.at[w_slot(2)], 2, [wb.at[1]])
        wc_copy.start()

    def w_f():
        wb_copy(0).wait_recv()
        wc_copy.wait_recv()
        w_add(dw_ref, 3, [wb.at[0], wc])

    def wl_copy(dh):
        to = lax.rem(hd + dh, nh)
        return remote(
            ow_any.at[:, pl.ds(pl.multiple_of(to * lw, 128), lw)], wl.at[dh - 1],
            l_s.at[dh - 1], l_r.at[dh - 1], {"head": to},
        )

    def o_copy(h, dh):
        return remote(
            oo.at[:, head(h)], oall.at[dh - 1, :, head(h)],
            o_s.at[h, dh - 1], o_r.at[h, dh - 1], {"head": lax.rem(hd + dh, nh)},
        )

    def layer_out():
        for dh in range(1, nh):
            wl_copy(dh).wait_recv()
            for h in range(heads):
                o_copy(h, dh).wait_recv()
        chunk = math.gcd(lw, 640)

        @pl.loop(0, lw // chunk)
        def _(j):
            at = pl.ds(pl.multiple_of(j * chunk, 128), chunk)
            mine = pl.ds(pl.multiple_of(hd * lw + j * chunk, 128), chunk)
            total = jnp.dot(oo[...], ow[:, mine], preferred_element_type=f32)
            for dh in range(1, nh):
                total += jnp.dot(oall[dh - 1], wl[dh - 1, :, at], preferred_element_type=f32)
            layer_ref[:, at] = total.astype(bf16)

    for h in range(heads):
        for i in (T_K, T_V, T_Q):
            for far in fars(i):
                move_start(i, h, far)
    for p in range(2):
        for dy in range(1, ny):
            gy_copy(p, dy, False).start()
        gc_copy(p, 0, False).start()

    if paired:
        g2x_copy().start()
    for dh in range(1, nh):
        wl_copy(dh).start()

    build_mask()
    own(0)
    own(1)
    own(2)
    fin(0)
    forward(0)
    g_relay(0)
    if paired:
        g2_turn()
    fin(1)
    forward(1)
    fin(2)
    forward(2)
    g_relay(1)
    d_attention()
    combine(0)
    combine(1)
    if paired:
        g2_relay()
    combine(2)
    w_parts()
    backward(0)
    w_b(1)
    w_b(0)
    backward(1)
    keys_sum(0)
    w_c()
    backward(2)
    keys_sum(1)
    layer_out()
    keys_sum(2)
    finish(0)
    finish(1)
    finish(2)
    w_f()

    for h in range(heads):
        for i in range(KINDS):
            for far in fars(i):
                move_sent(i, h, far)
        for k in range(2):
            for de in range(1, nx):
                a_copy(h, k, de, a_slot(k, de)).wait_send()
    for p in range(2):
        for dy in range(1, ny):
            gy_copy(p, dy, False).wait_send()
        for dy in range(ny):
            gc_copy(p, dy, False).wait_send()
    if paired:
        g2x_copy().wait_send()
        for dy in range(1, ny):
            g2y_copy(dy, False).wait_send()
        for dy in range(ny):
            g2c_copy(dy, False).wait_send()
        for h in range(heads):
            ox_copy(h).wait_send()
    else:
        for k in range(nz):
            for dx in range(1, nx):
                wx_copy(k, dx).wait_send()
    wb_copy(0).wait_send()
    wb_copy(1).wait_send()
    wc_copy.wait_send()
    for dh in range(1, nh):
        wl_copy(dh).wait_send()
        for h in range(heads):
            o_copy(h, dh).wait_send()


def layer(n_seq, nh, queries, keys, values, d_output, out_weight, lists):
    nz, nx = NZ, n_seq // NZ
    ny = nh // 2
    rows, width = queries.shape
    columns = out_weight.shape[1]
    heads, lw, share = width // HD, columns // nh, columns // n_seq
    dma = pltpu.SemaphoreType.DMA
    one = jax.ShapeDtypeStruct((rows, width), bf16)
    flat = pltpu.VMEM((rows, width), bf16)
    pair = (2, rows, HD)
    paired, tiny = nx == 2, pltpu.VMEM((16, 128), bf16)
    sems = [
        (heads, KINDS, 2), (heads,), (heads, 2, nx - 1),
        (heads, 2, nx - 1),
        (nz, nx - 1), (2,), (1,), (nh - 1,), (2, ny - 1), (2, ny),
        (heads, nh - 1), (1,), (ny - 1,), (ny,), (heads,),
    ]
    return pl.pallas_call(
        functools.partial(layer_kernel, nz, nx, nh),
        out_shape=(
            jax.ShapeDtypeStruct((rows, lw), bf16), one, one, one,
            jax.ShapeDtypeStruct((width, share), bf16),
        ),
        in_specs=[ANY] * 5 + [SMEM] * 3,
        out_specs=(VMEM,) * 5,
        scratch_shapes=[
            pltpu.VMEM((heads, 2 * nx) + pair, bf16),
            pltpu.VMEM((heads, 2 * rows, HD), bf16),
            pltpu.VMEM((heads, 2 * rows, HD), bf16),
            pltpu.VMEM((heads, 2, HD, rows), bf16),
            pltpu.VMEM((heads, 2, 8, rows), f32),
            pltpu.VMEM((heads, 2 * nx, 8, 2 * rows), f32),
            pltpu.VMEM((heads, 2 * nx, rows, 2 * rows), bf16),
            pltpu.VMEM((heads, 2, 8, rows), f32),
            pltpu.VMEM((heads, 8, rows), f32),
            pltpu.VMEM((heads, 2, HD, rows), bf16),
            pltpu.VMEM((heads, 2, 8, rows), f32),
            pltpu.VMEM((width, rows), bf16),
            flat,
            flat,
            pltpu.VMEM((width, rows), bf16),
            pltpu.VMEM((nh, rows, lw), bf16),
            pltpu.VMEM((width, columns), bf16),
            pltpu.VMEM((heads, 2, nx - 1) + pair, bf16),
            pltpu.VMEM((heads,) + pair, bf16),
            pltpu.VMEM((heads,) + pair, bf16),
            pltpu.VMEM((heads, 2) + pair, bf16),
            pltpu.VMEM((heads, 2) + pair, bf16),
            pltpu.VMEM((nz if paired else n_seq, width, share), bf16),
            tiny if paired else pltpu.VMEM((nz, nx - 1, width, share), bf16),
            pltpu.VMEM((2, width, share), bf16),
            pltpu.VMEM((width, share), bf16),
            pltpu.VMEM((nh - 1, width, lw), bf16),
            pltpu.VMEM((nh - 1, rows, width), bf16),
            pltpu.VMEM((nh, rows, share), bf16) if paired else tiny,
            pltpu.VMEM((width, rows), bf16) if paired else tiny,
            pltpu.VMEM((n_seq, PER_FRAME, 2 * rows), f32),
            pltpu.VMEM((rows, width), f32),
            pltpu.VMEM((HD, 2 * rows), f32),
        ]
        + [dma(s) for s in sems for _ in range(2)]
        + [dma((2,))],
        compiler_params=pltpu.CompilerParams(
            collective_id=0, has_side_effects=True, vmem_limit_bytes=60 * 2**20
        ),
    )(queries, keys, values, d_output, out_weight, *lists)


def on_device(
    n_seq, n_head,
    queries, keys, values, out_weight, d_output, block_keys, key_count, frame_slot,
):
    lists = (block_keys, key_count, frame_slot)
    return store(layer(n_seq, n_head, queries, keys, values, d_output, out_weight, lists))


def solution(mesh):
    return jax.shard_map(
        functools.partial(on_device, mesh.shape["seq"], mesh.shape["head"]),
        mesh=mesh,
        in_specs=(
            P("seq", "head"),
            P("seq", "head"),
            P("seq", "head"),
            P("head", None),
            P("seq", "head"),
            P(),
            P(),
            P(),
        ),
        out_specs=(
            P("seq", "head"),
            P("seq", "head"),
            P("seq", "head"),
            P("seq", "head"),
            P("head", "seq"),
        ),
        check_vma=False,
    )
```

```python
import functools
import math

import jax
import jax.numpy as jnp
from jax import lax
from jax.experimental import pallas as pl
from jax.experimental.pallas import tpu as pltpu
from jax.sharding import PartitionSpec as P

HD = 128
BLOCK = 128
FRAME_TOK = 384
PER_FRAME = FRAME_TOK // BLOCK
NZ = 4
NEG = -1e30
MESH = pl.DeviceIdType.MESH
VMEM = pl.BlockSpec(memory_space=pltpu.VMEM)
SMEM = pl.BlockSpec(memory_space=pltpu.SMEM)
ANY = pl.BlockSpec(memory_space=pl.ANY)
f32 = jnp.float32
bf16 = jnp.bfloat16
KINDS = 9
T_K, T_V, T_Q, T_G, T_STAT, T_OUT, T_LSE, T_DQ, T_DKV = range(KINDS)


def dot(a, b, ca, cb):
    return lax.dot_general(a, b, (((ca,), (cb,)), ((), ())), preferred_element_type=f32)


def store_kernel(n, *refs):
    sems = refs[2 * n]
    copies = [pltpu.make_async_copy(refs[i], refs[n + i], sems.at[i]) for i in range(n)]
    for c in copies:
        c.start()
    for c in copies:
        c.wait()


def store(arrays):
    n = len(arrays)
    return pl.pallas_call(
        functools.partial(store_kernel, n),
        out_shape=tuple(jax.ShapeDtypeStruct(a.shape, a.dtype) for a in arrays),
        in_specs=[VMEM] * n,
        out_specs=(ANY,) * n,
        scratch_shapes=[pltpu.SemaphoreType.DMA((n,))],
    )(*arrays)


def head(h):
    return slice(h * HD, (h + 1) * HD)


def place(nx):
    me, hd = lax.axis_index("seq"), lax.axis_index("head")
    z, x = me // nx, lax.rem(me, nx)
    xl, y, c = lax.rem(x, 2), hd // 2, lax.rem(hd, 2)
    e = x - xl + c
    return me, hd, z, x, xl, y, c, e


def layer_kernel(
    nz, nx, nh,
    q_any, k_any, v_any, dout_any, ow_any, keys_ref, count_ref, slot_ref,
    layer_ref, dq_ref, dk_ref, dv_ref, dw_ref,
    kv, qs, gs, os_ref, ls_ref, peak_ref, exps, stb, sto, opb, lsb, owt, oo, ga, gat,
    g_all, ow, ax, dqs, dqb, fin_ref, fb, wp, wx, wb, wc, wl, oall, g2, owtx, bias_ref, acc, acc_q,
    t_s, t_r, z1_s, z1_r, ec_s, ec_r,
    a_s, a_r, wx_s, wx_r, wb_s, wb_r, wc_s, wc_r, l_s, l_r,
    gy_s, gy_r, gc_s, gc_r, o_s, o_r, g2x_s, g2x_r, g2y_s, g2y_r, g2c_s, g2c_r, ox_s, ox_r, in_sem,
):
    me, hd, z, x, xl, y, c, e = place(nx)
    same = xl == c
    other = jnp.logical_not(same)
    rows, width = q_any.shape
    heads = width // HD
    n_seq = nz * nx
    ny = nh // 2
    lw = layer_ref.shape[1]
    share = dw_ref.shape[1]
    paired = nx == 2
    scale = 1.0 / math.sqrt(HD)
    z1 = z + 1 - 2 * lax.rem(z, 2)
    z2 = lax.rem(z + 2, nz)
    z3 = lax.rem(z1 + 2, nz)
    zs = (z1, z3, z2, z)
    core = y * 2 + 1 - c

    def dev(zz, ee):
        return {"seq": zz * nx + lax.div(ee, 2) * 2 + xl, "head": y * 2 + lax.rem(ee, 2)}

    def remote(src, dst, send, recv, device):
        return pltpu.make_async_remote_copy(
            src_ref=src, dst_ref=dst, send_sem=send, recv_sem=recv,
            device_id=device, device_id_type=MESH,
        )

    load_w = pltpu.make_async_copy(ow_any, ow, in_sem.at[0])
    load_g = pltpu.make_async_copy(dout_any, g_all.at[hd], in_sem.at[1])
    load_w.start()
    load_g.start()

    barrier = pltpu.get_barrier_semaphore()

    def greet(device):
        pl.semaphore_signal(barrier, inc=1, device_id=device, device_id_type=MESH)

    greet({"seq": z1 * nx + x})
    greet({"seq": z2 * nx + x})
    for dx in range(1, nx):
        greet({"seq": z * nx + lax.rem(x + dx, nx)})
    for dh in range(1, nh):
        greet({"head": lax.rem(hd + dh, nh)})

    for de in range(1, nx if nx > 2 else 1, 2):
        ee = lax.rem(e + de, nx)

        @pl.when(lax.div(ee, 2) != lax.div(e, 2))
        def _():
            greet(dev(z, ee))

    @pl.when(other)
    def _():
        for zz in (z, z1, z2):
            greet({"seq": zz * nx + e, "head": y * 2 + xl})

    peers = 2 + nx - 1 + nx // 2 - 1 + nh - 1
    pl.semaphore_wait(barrier, jnp.where(other, peers + 3, peers))

    def move_refs(i, h, far, landed):
        at = slice(h * HD, (h + 1) * HD)
        part = slice(far * rows, (far + 1) * rows)
        slot = e if landed else x
        return {
            T_K: lambda: (k_any.at[:, at], kv.at[h, slot, 0]),
            T_V: lambda: (v_any.at[:, at], kv.at[h, slot, 1]),
            T_Q: lambda: (q_any.at[:, at], qs.at[h, part, :]),
            T_G: lambda: (ga.at[:, at], gs.at[h, part, :]),
            T_STAT: lambda: (sto.at[h], stb.at[h, far]),
            T_OUT: lambda: (os_ref.at[h, far], opb.at[h, far]),
            T_LSE: lambda: (ls_ref.at[h, far], lsb.at[h, far]),
            T_DQ: lambda: (dqs.at[h, far], dqb.at[h, far]),
            T_DKV: lambda: (fin_ref.at[h, far], fb.at[h, far]),
        }[i]()

    def move(i, h, far, landed, local, away):
        src, dst = move_refs(i, h, far, landed)
        zz = z if far == 0 else (z1 if i == T_DKV else z2)
        device = {"seq": zz * nx + e, "head": y * 2 + xl}
        send, recv = t_s.at[h, i, far], t_r.at[h, i, far]
        if far:
            away(remote(src, dst, send, recv, device))
            return

        @pl.when(other)
        def _():
            away(remote(src, dst, send, recv, device))

        if local is not None:
            @pl.when(same)
            def _():
                local(pltpu.make_async_copy(src, dst, recv))

    def fars(i):
        return (0,) if i in (T_K, T_V) else (0, 1)

    def move_start(i, h, far):
        move(i, h, far, False, lambda d: d.start(), lambda d: d.start())

    def move_wait(i, h, far):
        move(i, h, far, True, lambda d: d.wait(), lambda d: d.wait_recv())

    def move_sent(i, h, far):
        move(i, h, far, False, None, lambda d: d.wait_send())

    def z1_copy(h):
        return remote(
            kv.at[h, e], kv.at[h, nx + e], z1_s.at[h], z1_r.at[h], dev(z1, e)
        )

    def e_copy(h, k, de, source):
        block = kv.at[h, k * nx + source]
        return remote(
            block, block, ec_s.at[h, k, de - 1], ec_r.at[h, k, de - 1],
            dev(z, lax.rem(e + de, nx)),
        )

    def own(h):
        move_wait(T_K, h, 0)
        move_wait(T_V, h, 0)
        z1_copy(h).start()
        for de in range(1, nx):
            e_copy(h, 0, de, e).start()

    def fin(h):
        z1_copy(h).wait_recv()
        for de in range(1, nx):
            e_copy(h, 1, de, e).start()
        for k in range(2):
            for de in range(1, nx):
                e_copy(h, k, de, lax.rem(e - de + nx, nx)).wait_recv()

    def gather_sent(h):
        z1_copy(h).wait_send()
        for k in range(2):
            for de in range(1, nx):
                e_copy(h, k, de, e).wait_send()

    half = rows // 2

    def part_of(ref, p):
        return ref.at[pl.ds(p * half, half), :]

    def gy_copy(p, dy, landed):
        block = lax.rem(y - dy + ny, ny) * 2 + c if landed else hd
        return remote(
            part_of(dout_any, p), g_all.at[block, pl.ds(p * half, half), :],
            gy_s.at[p, dy - 1], gy_r.at[p, dy - 1],
            {"head": lax.rem(y + dy, ny) * 2 + c},
        )

    def gc_copy(p, dy, landed):
        block = lax.rem(y - dy + ny, ny) * 2 + (1 - c if landed else c)
        dst = g_all.at[block, pl.ds(p * half, half), :]
        src = dst if dy else part_of(dout_any, p)
        return remote(src, dst, gc_s.at[p, dy], gc_r.at[p, dy], {"head": core})

    def g_relay(p):
        for dy in range(1, ny):
            gy_copy(p, dy, True).wait_recv()
            gc_copy(p, dy, False).start()

    def build_mask():
        shape = (n_seq, PER_FRAME, BLOCK)
        ids = lax.broadcasted_iota(jnp.int32, shape, 0) * PER_FRAME + lax.broadcasted_iota(
            jnp.int32, shape, 1
        )
        for i, zz in enumerate((z, z2)):
            logical = jnp.int32(0)
            for f in range(n_seq):
                logical = jnp.where(slot_ref[f] == zz * nx + e, jnp.int32(f), logical)
            for b in range(PER_FRAME):
                row = logical * PER_FRAME + b
                count = count_ref[row]

                def entry_step(j, bias):
                    entry = keys_ref[row, j]
                    f = lax.div(entry, PER_FRAME)
                    stored = slot_ref[f] * PER_FRAME + entry - f * PER_FRAME
                    return jnp.where(ids == jnp.where(j < count, stored, -1), 0.0, bias)

                at = slice(i * rows + b * BLOCK, i * rows + (b + 1) * BLOCK)
                bias_ref[:, :, at] = lax.fori_loop(
                    0, keys_ref.shape[1], entry_step, jnp.full(shape, NEG, f32)
                )

    def slot_frame(s):
        return jnp.where(s < nx, z * nx + s, z1 * nx + s - nx)

    def forward(h):
        move_wait(T_Q, h, 0)
        move_wait(T_Q, h, 1)
        factor = math.log2(math.e) / math.sqrt(HD)
        cols = 2 * rows

        def step(s, carry):
            peak, total, out = carry
            t = dot(kv[h, s, 0], qs[h], 1, 1).reshape(PER_FRAME, BLOCK, cols) * factor
            t = (t + bias_ref[slot_frame(s)][:, None, :]).reshape(rows, cols)
            top = jnp.max(jnp.max(t.reshape(rows // 8, 8, cols), axis=0), axis=0, keepdims=True)
            new = jnp.maximum(peak, top)
            less = jnp.exp2(peak - new)
            w = jnp.exp2(t - new)
            low = w.astype(bf16)
            exps[h, s] = low
            peak_ref[h, s] = jnp.broadcast_to(new, (8, cols))
            total = total * less + jnp.sum(w.reshape(rows // 8, 8, cols), axis=0)
            out = out * less + dot(kv[h, s, 1], low, 0, 0)
            return new, total, out

        peak, total, out = lax.fori_loop(
            0, 2 * nx, step,
            (jnp.full((1, cols), NEG, f32), jnp.zeros((8, cols), f32), jnp.zeros((HD, cols), f32)),
        )
        total = jnp.sum(total, axis=0, keepdims=True)
        out = (out * (1.0 / total)).astype(bf16)
        lse = jnp.broadcast_to(peak + jnp.log2(total), (8, cols))
        for far in range(2):
            os_ref[h, far] = out[:, far * rows:(far + 1) * rows]
            ls_ref[h, far] = lse[:, far * rows:(far + 1) * rows]
            move_start(T_OUT, h, far)
            move_start(T_LSE, h, far)

    def combine(h):
        for far in range(2):
            move_wait(T_OUT, h, far)
            move_wait(T_LSE, h, far)
        one, two = lsb[h, 0, 0:1, :], lsb[h, 1, 0:1, :]
        top = jnp.maximum(one, two)
        lse = top + jnp.log2(jnp.exp2(one - top) + jnp.exp2(two - top))
        out = opb[h, 0].astype(f32) * jnp.exp2(one - lse) + opb[h, 1].astype(f32) * jnp.exp2(two - lse)
        low = out.astype(bf16)
        owt[head(h), :] = low
        oo[:, head(h)] = out.T.astype(bf16)
        sto[h] = jnp.broadcast_to(lse, (8, rows))
        if paired:
            ox_copy(h).start()
        for dh in range(1, nh):
            o_copy(h, dh).start()

    def send_stat(h):
        delta = jnp.sum(
            gat[head(h), :].astype(f32) * owt[head(h), :].astype(f32), axis=0, keepdims=True
        )
        sub = lax.broadcasted_iota(jnp.int32, (8, rows), 0)
        sto[h] = jnp.where(sub < 4, sto[h], delta)
        move_start(T_STAT, h, 0)
        move_start(T_STAT, h, 1)

    def d_attention():
        for p in range(2):
            for dy in range(ny):
                gc_copy(p, dy, True).wait_recv()
        load_g.wait()
        load_w.wait()
        acc[...] = jnp.zeros_like(acc)

        @pl.loop(0, nh)
        def _(j):
            acc[...] += dot(g_all[j], ow[:, pl.ds(pl.multiple_of(j * lw, 128), lw)], 1, 1)

        ga[...] = acc[...].astype(bf16)
        for h in range(heads):
            move_start(T_G, h, 0)
            move_start(T_G, h, 1)
        gat[...] = acc[...].T.astype(bf16)

    def a_copy(h, k, de, s):
        return remote(
            kv.at[h, s], ax.at[h, k, de - 1], a_s.at[h, k, de - 1], a_r.at[h, k, de - 1],
            dev(z, lax.rem(e + de, nx)),
        )

    def a_slot(k, de):
        return k * nx + lax.rem(e + de, nx)

    def backward(h):
        gather_sent(h)
        for far in range(2):
            move_wait(T_G, h, far)
            move_wait(T_STAT, h, far)
        lse = jnp.concatenate([stb[h, 0, 0:1, :], stb[h, 1, 0:1, :]], axis=1)
        delta = jnp.concatenate([stb[h, 0, 4:5, :], stb[h, 1, 4:5, :]], axis=1)
        acc_q[...] = jnp.zeros_like(acc_q)

        @pl.loop(0, 2 * nx)
        def _(u):
            k = 1 - u // nx
            de = lax.rem(lax.rem(u, nx) + 1, nx)
            s = k * nx + lax.rem(e + de, nx)
            q, g = qs[h], gs[h]
            kb, vb = kv[h, s, 0], kv[h, s, 1]
            w = exps[h, s].astype(f32) * jnp.exp2(peak_ref[h, s, 0:1, :] - lse)
            ds = (w * (dot(vb, g, 1, 1) - delta)).astype(bf16)
            kv[h, s, 1] = dot(w.astype(bf16), g, 1, 0).astype(bf16)
            kv[h, s, 0] = dot(ds, q, 1, 0).astype(bf16)
            acc_q[...] += dot(kb, ds, 0, 0)

            @pl.when(de > 0)
            def _():
                a_copy(h, k, de, s).start()

        for far in range(2):
            dqs[h, far] = acc_q[:, far * rows:(far + 1) * rows].T.astype(bf16)
            move_start(T_DQ, h, far)

    def add_up(out, terms, factor=1.0):
        @pl.loop(0, rows // BLOCK)
        def _(r):
            at = pl.ds(pl.multiple_of(r * BLOCK, BLOCK), BLOCK)
            total = terms[0][at, :].astype(f32)
            for t in terms[1:]:
                total += t[at, :].astype(f32)
            out[at, :] = (total * factor).astype(bf16)

    def keys_sum(h):
        for k in (1, 0):
            for de in range(1, nx):
                a_copy(h, k, de, a_slot(k, de)).wait_recv()
            for i in range(2):
                add_up(
                    fin_ref.at[h, k, i],
                    [kv.at[h, k * nx + e, i]] + [ax.at[h, k, de - 1, i] for de in range(1, nx)],
                )
            move_start(T_DKV, h, k)

    def finish(h):
        at = head(h)
        for far in range(2):
            move_wait(T_DQ, h, far)
        add_up(dq_ref.at[:, at], [dqb.at[h, 0], dqb.at[h, 1]], scale)
        for far in range(2):
            move_wait(T_DKV, h, far)
        add_up(dk_ref.at[:, at], [fb.at[h, 0, 0], fb.at[h, 1, 0]], scale)
        add_up(dv_ref.at[:, at], [fb.at[h, 0, 1], fb.at[h, 1, 1]])

    def ox_copy(h):
        return remote(
            owt.at[head(h), :], owtx.at[head(h), :], ox_s.at[h], ox_r.at[h],
            {"seq": z * nx + nx - 1 - x},
        )

    def g2x_copy():
        px = nx - 1 - x
        at = pl.ds(pl.multiple_of(px * share, 128), share)
        return remote(
            dout_any.at[:, at], g2.at[hd], g2x_s.at[0], g2x_r.at[0], {"seq": z * nx + px}
        )

    def g2y_copy(dy, landed):
        block = lax.rem(y - dy + ny, ny) * 2 + c if landed else hd
        return remote(
            g2.at[block], g2.at[block], g2y_s.at[dy - 1], g2y_r.at[dy - 1],
            {"head": lax.rem(y + dy, ny) * 2 + c},
        )

    def g2c_copy(dy, landed):
        block = g2.at[lax.rem(y - dy + ny, ny) * 2 + (1 - c if landed else c)]
        return remote(block, block, g2c_s.at[dy], g2c_r.at[dy], {"head": core})

    def g2_turn():
        g2x_copy().wait_recv()
        for dy in range(1, ny):
            g2y_copy(dy, False).start()
        g2c_copy(0, False).start()

    def g2_relay():
        for dy in range(1, ny):
            g2y_copy(dy, True).wait_recv()
            g2c_copy(dy, False).start()

    def wx_copy(k, dx):
        px = lax.rem(x + dx, nx)
        return remote(
            wp.at[zs[k] * nx + px], wx.at[k, dx - 1], wx_s.at[k, dx - 1], wx_r.at[k, dx - 1],
            {"seq": z * nx + px},
        )

    def w_slot(k):
        return k if paired else zs[k] * nx + x

    def wb_copy(k):
        return remote(
            wp.at[w_slot(k)], wb.at[k], wb_s.at[k], wb_r.at[k], {"seq": z1 * nx + x}
        )

    wc_copy = remote(wp.at[w_slot(2)], wc, wc_s.at[0], wc_r.at[0], {"seq": z2 * nx + x})
    per = lw // share

    def w_pair(k):
        p = zs[k] * nx + x
        at = pl.ds(pl.multiple_of(lax.rem(p, per) * share, 128), share)
        block = lax.div(p, per)
        wp[k] = (
            jnp.dot(owt[...], g_all[block, :, at], preferred_element_type=f32)
            + jnp.dot(owtx[...], g2[block], preferred_element_type=f32)
        ).astype(bf16)

    def w_parts():
        if paired:
            for dy in range(ny):
                g2c_copy(dy, True).wait_recv()
            for h in range(heads):
                ox_copy(h).wait_recv()
            for k in (1, 0):
                w_pair(k)
                wb_copy(k).start()
            for k in (2, 3):
                w_pair(k)
            return

        @pl.loop(0, nh)
        def _(j):
            r = jnp.dot(owt[...], g_all[j], preferred_element_type=f32).astype(bf16)
            for t in range(per):
                wp[j * per + t] = r[:, t * share:(t + 1) * share]

        for k in range(nz):
            for dx in range(1, nx):
                wx_copy(k, dx).start()

    def w_add(out, k, extra):
        slot = w_slot(k)
        if not paired:
            for dx in range(1, nx):
                wx_copy(k, dx).wait_recv()

        @pl.loop(0, width // BLOCK)
        def _(r):
            at = pl.ds(pl.multiple_of(r * BLOCK, BLOCK), BLOCK)
            total = wp[slot, at, :].astype(f32)
            if not paired:
                for dx in range(1, nx):
                    total += wx[k, dx - 1, at, :].astype(f32)
            for t in extra:
                total += t[at, :].astype(f32)
            out[at, :] = total.astype(bf16)

    def w_b(k):
        if not paired:
            w_add(wp.at[w_slot(k)], k, [])
            wb_copy(k).start()

    def w_c():
        wb_copy(1).wait_recv()
        w_add(wp.at[w_slot(2)], 2, [wb.at[1]])
        wc_copy.start()

    def w_f():
        wb_copy(0).wait_recv()
        wc_copy.wait_recv()
        w_add(dw_ref, 3, [wb.at[0], wc])

    def wl_copy(dh):
        to = lax.rem(hd + dh, nh)
        return remote(
            ow_any.at[:, pl.ds(pl.multiple_of(to * lw, 128), lw)], wl.at[dh - 1],
            l_s.at[dh - 1], l_r.at[dh - 1], {"head": to},
        )

    def o_copy(h, dh):
        return remote(
            oo.at[:, head(h)], oall.at[dh - 1, :, head(h)],
            o_s.at[h, dh - 1], o_r.at[h, dh - 1], {"head": lax.rem(hd + dh, nh)},
        )

    def layer_out():
        for dh in range(1, nh):
            wl_copy(dh).wait_recv()
            for h in range(heads):
                o_copy(h, dh).wait_recv()
        chunk = math.gcd(lw, 640)

        @pl.loop(0, lw // chunk)
        def _(j):
            at = pl.ds(pl.multiple_of(j * chunk, 128), chunk)
            mine = pl.ds(pl.multiple_of(hd * lw + j * chunk, 128), chunk)
            total = jnp.dot(oo[...], ow[:, mine], preferred_element_type=f32)
            for dh in range(1, nh):
                total += jnp.dot(oall[dh - 1], wl[dh - 1, :, at], preferred_element_type=f32)
            layer_ref[:, at] = total.astype(bf16)

    for h in range(heads):
        for i in (T_K, T_V, T_Q):
            for far in fars(i):
                move_start(i, h, far)
    for p in range(2):
        for dy in range(1, ny):
            gy_copy(p, dy, False).start()
        gc_copy(p, 0, False).start()
    build_mask()
    own(0)
    own(1)
    own(2)
    if paired:
        g2x_copy().start()
    fin(0)
    forward(0)
    g_relay(0)
    fin(1)
    forward(1)
    fin(2)
    forward(2)
    g_relay(1)
    if paired:
        g2_turn()
    d_attention()
    combine(0)
    combine(1)
    combine(2)
    for h in range(heads):
        send_stat(h)
    if paired:
        g2_relay()
    for dh in range(1, nh):
        wl_copy(dh).start()
    w_parts()
    backward(0)
    w_b(1)
    w_b(0)
    backward(1)
    keys_sum(0)
    w_c()
    backward(2)
    keys_sum(1)
    keys_sum(2)
    layer_out()
    finish(0)
    finish(1)
    finish(2)
    w_f()

    for h in range(heads):
        for i in range(KINDS):
            for far in fars(i):
                move_sent(i, h, far)
        for k in range(2):
            for de in range(1, nx):
                a_copy(h, k, de, a_slot(k, de)).wait_send()
    for p in range(2):
        for dy in range(1, ny):
            gy_copy(p, dy, False).wait_send()
        for dy in range(ny):
            gc_copy(p, dy, False).wait_send()
    if paired:
        g2x_copy().wait_send()
        for dy in range(1, ny):
            g2y_copy(dy, False).wait_send()
        for dy in range(ny):
            g2c_copy(dy, False).wait_send()
        for h in range(heads):
            ox_copy(h).wait_send()
    else:
        for k in range(nz):
            for dx in range(1, nx):
                wx_copy(k, dx).wait_send()
    wb_copy(0).wait_send()
    wb_copy(1).wait_send()
    wc_copy.wait_send()
    for dh in range(1, nh):
        wl_copy(dh).wait_send()
        for h in range(heads):
            o_copy(h, dh).wait_send()


def layer(n_seq, nh, queries, keys, values, d_output, out_weight, lists):
    nz, nx = NZ, n_seq // NZ
    ny = nh // 2
    rows, width = queries.shape
    columns = out_weight.shape[1]
    heads, lw, share = width // HD, columns // nh, columns // n_seq
    dma = pltpu.SemaphoreType.DMA
    one = jax.ShapeDtypeStruct((rows, width), bf16)
    flat = pltpu.VMEM((rows, width), bf16)
    pair = (2, rows, HD)
    paired, tiny = nx == 2, pltpu.VMEM((16, 128), bf16)
    sems = [
        (heads, KINDS, 2), (heads,), (heads, 2, nx - 1),
        (heads, 2, nx - 1),
        (nz, nx - 1), (2,), (1,), (nh - 1,), (2, ny - 1), (2, ny),
        (heads, nh - 1), (1,), (ny - 1,), (ny,), (heads,),
    ]
    return pl.pallas_call(
        functools.partial(layer_kernel, nz, nx, nh),
        out_shape=(
            jax.ShapeDtypeStruct((rows, lw), bf16), one, one, one,
            jax.ShapeDtypeStruct((width, share), bf16),
        ),
        in_specs=[ANY] * 5 + [SMEM] * 3,
        out_specs=(VMEM,) * 5,
        scratch_shapes=[
            pltpu.VMEM((heads, 2 * nx) + pair, bf16),
            pltpu.VMEM((heads, 2 * rows, HD), bf16),
            pltpu.VMEM((heads, 2 * rows, HD), bf16),
            pltpu.VMEM((heads, 2, HD, rows), bf16),
            pltpu.VMEM((heads, 2, 8, rows), f32),
            pltpu.VMEM((heads, 2 * nx, 8, 2 * rows), f32),
            pltpu.VMEM((heads, 2 * nx, rows, 2 * rows), bf16),
            pltpu.VMEM((heads, 2, 8, rows), f32),
            pltpu.VMEM((heads, 8, rows), f32),
            pltpu.VMEM((heads, 2, HD, rows), bf16),
            pltpu.VMEM((heads, 2, 8, rows), f32),
            pltpu.VMEM((width, rows), bf16),
            flat,
            flat,
            pltpu.VMEM((width, rows), bf16),
            pltpu.VMEM((nh, rows, lw), bf16),
            pltpu.VMEM((width, columns), bf16),
            pltpu.VMEM((heads, 2, nx - 1) + pair, bf16),
            pltpu.VMEM((heads,) + pair, bf16),
            pltpu.VMEM((heads,) + pair, bf16),
            pltpu.VMEM((heads, 2) + pair, bf16),
            pltpu.VMEM((heads, 2) + pair, bf16),
            pltpu.VMEM((nz if paired else n_seq, width, share), bf16),
            tiny if paired else pltpu.VMEM((nz, nx - 1, width, share), bf16),
            pltpu.VMEM((2, width, share), bf16),
            pltpu.VMEM((width, share), bf16),
            pltpu.VMEM((nh - 1, width, lw), bf16),
            pltpu.VMEM((nh - 1, rows, width), bf16),
            pltpu.VMEM((nh, rows, share), bf16) if paired else tiny,
            pltpu.VMEM((width, rows), bf16) if paired else tiny,
            pltpu.VMEM((n_seq, PER_FRAME, 2 * rows), f32),
            pltpu.VMEM((rows, width), f32),
            pltpu.VMEM((HD, 2 * rows), f32),
        ]
        + [dma(s) for s in sems for _ in range(2)]
        + [dma((2,))],
        compiler_params=pltpu.CompilerParams(
            collective_id=0, has_side_effects=True, vmem_limit_bytes=60 * 2**20
        ),
    )(queries, keys, values, d_output, out_weight, *lists)


def on_device(
    n_seq, n_head,
    queries, keys, values, out_weight, d_output, block_keys, key_count, frame_slot,
):
    lists = (block_keys, key_count, frame_slot)
    return store(layer(n_seq, n_head, queries, keys, values, d_output, out_weight, lists))


def solution(mesh):
    return jax.shard_map(
        functools.partial(on_device, mesh.shape["seq"], mesh.shape["head"]),
        mesh=mesh,
        in_specs=(
            P("seq", "head"),
            P("seq", "head"),
            P("seq", "head"),
            P("head", None),
            P("seq", "head"),
            P(),
            P(),
            P(),
        ),
        out_specs=(
            P("seq", "head"),
            P("seq", "head"),
            P("seq", "head"),
            P("seq", "head"),
            P("head", "seq"),
        ),
        check_vma=False,
    )
```
